256 devices in a mesh: rows: 128 (over y, z, x), blk: 2 (over core).
Axes of the slice: x: 4, y: 4, z: 8, core: 2. Of those that a mesh axis runs over, the one named last changes fastest.
Arguments:
- inputs: bfloat16 [131072, 440], P('rows'), may hold values from -6 to 6
- proj: bfloat16 [4, 440, 512], P('blk'), may hold values from -0.25 to 0.25
- phase: bfloat16 [4, 512], P('blk'), may hold values from -3.140625 to 3.140625
- targets: bfloat16 [131072, 1024], P('rows', 'blk'), may hold values from -6 to 6
Outputs:
- coefs: float32 [4, 512, 1024], P(None, None, 'blk')
- residual: float32 [131072, 1024], P('rows', 'blk')
The draws below stay inside these ranges and needn't reach their ends.
All inputs are finite; a program needn't handle non-finite values.
Results may differ from the reference program's by a relative error of at most 0.0035.
The reference program's roundings to bfloat16 on the way count: a program that leaves them out, or rounds other values in their place, can miss the bound.
Values may be sent and summed in bfloat16 or wider, within the bound.
A program may use at most 128 MiB of HBM per device.

```python
import math
import jax
import jax.numpy as jnp
from jax import lax

DIN = 440
F = 512
ROWS = 131072
NBLK = 4
TGT = 1024


def shard_levels(stream_key, extent, split, smallest, top_value):
    def one(position, parts):
        heights = jax.random.uniform(jax.random.fold_in(jax.random.fold_in(stream_key, 6), position), (parts,), jnp.float32, smallest / len(split), top_value / len(split))
        return jnp.repeat(jnp.exp(heights), extent[position] // parts).reshape((-1,) + (1,) * (len(extent) - position - 1))

    gain = one(*split[0])
    for cut in split[1:]:
        gain = gain * one(*cut)
    return gain


def centred(own_key, shape, width, bound, cuts=(), kind=jnp.bfloat16):
    result = width * jax.random.normal(own_key, shape, jnp.float32)
    if cuts:
        result = result * shard_levels(own_key, shape, cuts, -0.22, 0.18)
    return jnp.clip(result, -bound, bound).astype(kind)


def setup_inputs(seed: int = 0) -> dict:
    arg_keys = jax.random.split(jax.random.key(seed), 5)
    inputs = centred(arg_keys[0], (ROWS, DIN), 1.0, 6.0, ((0, 128),))
    proj = centred(arg_keys[1], (NBLK, DIN, F), DIN ** -0.5, 0.25, ((0, 2),))
    phase = jnp.clip(jax.random.uniform(arg_keys[2], (NBLK, F), jnp.float32, -3.140625, 3.140625), -3.140625, 3.140625).astype(jnp.bfloat16)
    targets = centred(arg_keys[3], (ROWS, TGT), 1.0, 6.0, ((0, 128), (1, 2)))
    return dict(inputs=inputs, proj=proj, phase=phase, targets=targets)


ridge = 0.05

def features(inputs, weights, shift):
    pre = jnp.dot(inputs.astype(jnp.float32), weights.astype(jnp.float32), preferred_element_type=jnp.float32) + shift.astype(jnp.float32)
    return (jnp.cos(pre) * (1.0 / math.sqrt(ROWS))).astype(jnp.bfloat16)

def reference(inputs, proj, phase, targets):
    identity_mat = jnp.eye(F, dtype=jnp.float32)
    factor_list = []
    for block in range(NBLK):
        feats = features(inputs, proj[block], phase[block])
        gram = lax.dot_general(feats.astype(jnp.float32), feats.astype(jnp.float32), (((0,), (0,)), ((), ())), preferred_element_type=jnp.float32)
        factor_list.append(jnp.linalg.cholesky(gram + ridge * identity_mat))
    residual = targets.astype(jnp.float32)
    coef_list = []
    for block in range(NBLK):
        feats = features(inputs, proj[block], phase[block])
        corr = lax.dot_general(feats.astype(jnp.float32), residual.astype(jnp.bfloat16).astype(jnp.float32), (((0,), (0,)), ((), ())), preferred_element_type=jnp.float32)
        delta = jax.scipy.linalg.cho_solve((factor_list[block], True), corr)
        coef_list.append(delta)
        residual = residual - jnp.dot(feats.astype(jnp.float32), delta.astype(jnp.bfloat16).astype(jnp.float32), preferred_element_type=jnp.float32)
    return (jnp.stack(coef_list), residual)
```

```python
import functools
import math

import jax
import jax.numpy as jnp
from jax import lax
from jax.experimental import pallas as pl
from jax.experimental.pallas import tpu as pltpu
from jax.sharding import PartitionSpec as P

MESH = pl.DeviceIdType.MESH
HIGHEST = lax.Precision.HIGHEST
ridge = 0.05

F = 512
LANES = 128
SLABS = F // LANES
BLOCKS = 9
DATA_ROWS = BLOCKS * SLABS * F

AXES = ((4, 32), (4, 8), (8, 1))


def coords():
    r = lax.axis_index("rows")
    return r, [lax.rem(r // stride, n) for n, stride in AXES]


def sibling():
    return {"blk": 1 - lax.axis_index("blk")}


COS_COEFS = None


def cos_turns(t):
    u = jnp.abs(t) - 0.25
    w = u * u
    acc = jnp.full_like(w, SIN_POLY[-1])
    for coef in SIN_POLY[-2::-1]:
        acc = acc * w + coef
    return acc * u


def fit_sin_poly():
    import numpy as np

    degree = 5
    nodes = (np.cos((np.arange(degree + 1) + 0.5) * np.pi / (degree + 1)) + 1.0) / 32.0
    root = np.sqrt(nodes)
    values = -np.sin(2 * np.pi * root) / root
    vander = np.vander(nodes, degree + 1, increasing=True)
    return [float(v) for v in np.linalg.solve(vander, values)]


SIN_POLY = fit_sin_poly()


def feature_kernel(scale, x_ref, projt_ref, phase_ref, y_ref, ft_ref, part_ref, send_sem, recv_sem):
    core = lax.axis_index("blk")
    rows = x_ref.shape[0]
    barrier = pltpu.get_barrier_semaphore()
    pl.semaphore_signal(barrier, inc=1, device_id=sibling(), device_id_type=MESH)
    pl.semaphore_wait(barrier, 1)

    chunk = 256
    copies = []
    for i in range(2):
        g = 2 * core + i

        def piece(j, _, i=i, g=g):
            cols = pl.ds(pl.multiple_of(j * chunk, chunk), chunk)
            pre = lax.dot_general(
                projt_ref[i], x_ref[cols, :], (((1,), (1,)), ((), ())), preferred_element_type=jnp.float32
            )
            turns = (pre + phase_ref[i]) * (0.5 / math.pi)
            turns = turns - jnp.round(turns)
            ft_ref[g, :, cols] = (cos_turns(turns) * scale).astype(jnp.bfloat16)
            return 0

        lax.fori_loop(0, rows // chunk, piece, 0)
        copy = pltpu.make_async_remote_copy(
            src_ref=ft_ref.at[g],
            dst_ref=ft_ref.at[g],
            send_sem=send_sem.at[i],
            recv_sem=recv_sem.at[i],
            device_id=sibling(),
            device_id_type=MESH,
        )
        copy.start()
        copies.append(copy)

    def put(q, half, value):
        for k in range(2):
            row = pl.multiple_of((q * SLABS + 2 * half + k) * F, F)
            part_ref[pl.ds(row, F), :] = value[:, k * LANES:(k + 1) * LANES]

    def gram(q, a, b):
        def one(half, _):
            cols = pl.ds(pl.multiple_of(half * 256, 256), 256)
            put(q, half, lax.dot_general(
                ft_ref[a], ft_ref[b, cols, :], (((1,), (1,)), ((), ())), preferred_element_type=jnp.float32
            ))
            return 0

        lax.fori_loop(0, 2, one, 0)

    def moment(b):
        def one(half, _):
            cols = pl.ds(pl.multiple_of(half * 256, 256), 256)
            put(5 + b, half, jnp.dot(ft_ref[b], y_ref[:, cols], preferred_element_type=jnp.float32))
            return 0

        lax.fori_loop(0, 2, one, 0)

    own = [2 * core, 2 * core + 1]
    other = [2 * (1 - core), 2 * (1 - core) + 1]
    gram(0, own[0], own[0])
    gram(1, own[1], own[1])
    gram(2, own[1], own[0])
    moment(own[0])
    moment(own[1])
    for i in range(2):
        pltpu.make_async_remote_copy(
            src_ref=ft_ref.at[own[i]],
            dst_ref=ft_ref.at[other[i]],
            send_sem=send_sem.at[i],
            recv_sem=recv_sem.at[i],
            device_id=sibling(),
            device_id_type=MESH,
        ).wait_recv()
    gram(3, 2, core)
    gram(4, 3, 1 - core)
    moment(other[0])
    moment(other[1])
    for copy in copies:
        copy.wait_send()


def features_and_parts(x, projt, phase, y):
    rows = x.shape[0]
    scale = 1.0 / math.sqrt(rows * 128)
    vmem = pl.BlockSpec(memory_space=pltpu.VMEM)
    return pl.pallas_call(
        functools.partial(feature_kernel, scale),
        out_shape=(
            jax.ShapeDtypeStruct((4, F, rows), jnp.bfloat16),
            jax.ShapeDtypeStruct((DATA_ROWS, LANES), jnp.float32),
        ),
        in_specs=[vmem] * 4,
        out_specs=(vmem, vmem),
        scratch_shapes=[pltpu.SemaphoreType.DMA((2,)), pltpu.SemaphoreType.DMA((2,))],
        compiler_params=pltpu.CompilerParams(
            collective_id=0, has_side_effects=True, vmem_limit_bytes=60 * 2**20
        ),
        name="features",
    )(x, projt, phase, y)


class Stream:
    def __init__(self, index, part, direction, base, length):
        self.index, self.dir, self.base = index, direction, base
        self.order = [(part + t) % 3 for t in range(3)]
        self.sizes = [AXES[a][0] for a in self.order]
        self.rows = []
        for n in self.sizes:
            length //= n
            self.rows.append(length)
        slot = base
        self.steps = []
        for t in range(3):
            for s in range(self.sizes[t] - 1):
                self.steps.append(("sum", t, s, slot))
                slot += self.rows[t]
        for t in (2, 1, 0):
            for s in range(self.sizes[t] - 1):
                self.steps.append(("gather", t, s, None))

    def slot_of(self, t, s):
        for kind, tt, ss, slot in self.steps:
            if kind == "sum" and (tt, ss) == (t, s):
                return slot


def add_rows(dst, dst_off, src, src_off, rows):
    step = rows
    for cand in (192, 128, 96):
        if rows > cand and rows % cand == 0:
            step = cand
            break
    if step == rows:
        dst[pl.ds(dst_off, rows), :] = dst[pl.ds(dst_off, rows), :] + src[pl.ds(src_off, rows), :]
        return

    def one(j, _):
        d = pl.ds(pl.multiple_of(dst_off + j * step, 8), step)
        s = pl.ds(pl.multiple_of(src_off + j * step, 8), step)
        dst[d, :] = dst[d, :] + src[s, :]
        return 0

    lax.fori_loop(0, rows // step, one, 0)


def plan(streams):
    events = []
    for st in streams:
        time = 0.0
        for k, (kind, t, s, slot) in enumerate(st.steps):
            time += 2.0 + st.rows[t] * LANES * 4 * 2 / 90e3
            events.append((time, st.index, k))
    return sorted(events)


def ring_kernel(streams, data_ref, out_ref, held, send_sem, recv_sem):
    r, here = coords()
    barrier = pltpu.get_barrier_semaphore()

    def neighbour(axis, direction):
        n, stride = AXES[axis]
        return {"rows": r + (lax.rem(here[axis] + n + direction, n) - here[axis]) * stride}

    for axis in range(3):
        for direction in (1, -1):
            pl.semaphore_signal(barrier, inc=1, device_id=neighbour(axis, direction), device_id_type=MESH)
    pl.semaphore_wait(barrier, 6)

    def aligned(v):
        return v if isinstance(v, int) else pl.multiple_of(v, 8)

    def chunk(st, t, back):
        n = st.sizes[t]
        return lax.rem(here[st.order[t]] - st.dir * back + 4 * n, n)

    def own_rows(st, t, k):
        if t == 0:
            return data_ref, aligned(st.base + k * st.rows[0])
        return held, aligned(st.slot_of(t - 1, st.sizes[t - 1] - 2) + k * st.rows[t])

    def out_rows(st, t, k):
        off = st.base
        for tt in range(t):
            off = off + here[st.order[tt]] * st.rows[tt]
        return aligned(off + k * st.rows[t])

    def make(st, k, receive=False):
        kind, t, s, slot = st.steps[k]
        rows = st.rows[t]
        axis = st.order[t]
        if kind == "sum":
            if s == 0:
                src, off = own_rows(st, t, chunk(st, t, 1))
            else:
                src, off = held, st.slot_of(t, s - 1)
            source = src.at[pl.ds(off, rows), :]
            dest = held.at[pl.ds(slot, rows), :]
        else:
            at = out_rows(st, t, chunk(st, t, s))
            if t == 2 and s == 0:
                source = held.at[pl.ds(st.slot_of(2, st.sizes[2] - 2), rows), :]
            else:
                source = out_ref.at[pl.ds(at, rows), :]
            if receive:
                at = out_rows(st, t, chunk(st, t, s + 1))
            dest = out_ref.at[pl.ds(at, rows), :]
        return pltpu.make_async_remote_copy(
            src_ref=source,
            dst_ref=dest,
            send_sem=send_sem.at[st.index, k],
            recv_sem=recv_sem.at[st.index, k],
            device_id=neighbour(axis, st.dir),
            device_id_type=MESH,
        )

    for st in streams:
        make(st, 0).start()
    for _, index, k in plan(streams):
        st = streams[index]
        kind, t, s, slot = st.steps[k]
        make(st, k, receive=True).wait_recv()
        if kind == "sum":
            src, off = own_rows(st, t, chunk(st, t, s + 2))
            add_rows(held, slot, src, off, st.rows[t])
        if k + 1 < len(st.steps):
            make(st, k + 1).start()
        if kind == "sum" and t == 2 and s == st.sizes[2] - 2:
            at = out_rows(st, 2, here[st.order[2]])
            out_ref[pl.ds(at, st.rows[2]), :] = held[pl.ds(slot, st.rows[2]), :]
    for st in streams:
        for k in range(len(st.steps)):
            make(st, k).wait_send()


def ring_sum(data):
    total = data.shape[0]
    length = total // 6
    streams = [Stream(2 * p + d, p, (1, -1)[d], (2 * p + d) * length, length) for p in range(3) for d in range(2)]
    nsteps = len(streams[0].steps)
    vmem = pl.BlockSpec(memory_space=pltpu.VMEM)
    return pl.pallas_call(
        functools.partial(ring_kernel, streams),
        out_shape=jax.ShapeDtypeStruct(data.shape, jnp.float32),
        in_specs=[vmem],
        out_specs=vmem,
        scratch_shapes=[
            pltpu.VMEM(data.shape, jnp.float32),
            pltpu.SemaphoreType.DMA((len(streams), nsteps)),
            pltpu.SemaphoreType.DMA((len(streams), nsteps)),
        ],
        compiler_params=pltpu.CompilerParams(
            collective_id=1, has_side_effects=True, vmem_limit_bytes=60 * 2**20
        ),
        name="ring_sum",
    )(data)


LOW, HIGH_EIG = 0.05, 130.0
NEWTON = 8


def base_inverses(mats):
    n = mats[0].shape[0]
    eye = (
        lax.broadcasted_iota(jnp.int32, (n, n), 0) == lax.broadcasted_iota(jnp.int32, (n, n), 1)
    ).astype(jnp.float32)
    c = 2.0 / (LOW + HIGH_EIG)
    rho = (HIGH_EIG - LOW) / (HIGH_EIG + LOW)

    def grow(rho):
        return rho * rho / (2.0 - rho * rho)

    s = 2.0 / (2.0 - rho * rho)
    xs = [s * (2.0 * c * eye - (c * c) * m) for m in mats]
    rho = grow(rho)

    def step(_, carry):
        xs, rho = carry
        s = 2.0 / (2.0 - rho * rho)
        nxt = []
        for m, x in zip(mats, xs):
            ax = jnp.dot(m, x, precision=HIGHEST, preferred_element_type=jnp.float32)
            xax = jnp.dot(x, ax, precision=HIGHEST, preferred_element_type=jnp.float32)
            nxt.append(s * (2.0 * x - xax))
        return tuple(nxt), rho * rho / (2.0 - rho * rho)

    xs, _ = lax.fori_loop(0, NEWTON, step, (tuple(xs), jnp.float32(rho)))
    return xs


def inverse_kernel(g_ref, out_ref):
    p = LANES
    for m in range(2):
        for k in range(SLABS):
            slab = g_ref[pl.ds((m * SLABS + k) * F, F), :]
            row = lax.broadcasted_iota(jnp.int32, (F, p), 0)
            col = lax.broadcasted_iota(jnp.int32, (F, p), 1) + k * p
            out_ref[m, :, k * p:(k + 1) * p] = jnp.where(row == col, slab + ridge, slab)
    for k in range(F // p):
        here = slice(k * p, (k + 1) * p)
        pivots = base_inverses([out_ref[m, here, here] for m in range(2)])
        for m in range(2):
            row = jnp.dot(pivots[m], out_ref[m, here, :], precision=HIGHEST, preferred_element_type=jnp.float32)
            col = out_ref[m, :, here]
            out_ref[m, :, here] = jnp.zeros_like(col)
            out_ref[m, here, :] = row
            out_ref[m, here, here] = pivots[m]
            full = out_ref[m, here, :]
            for i in range(F // p):
                if i != k:
                    rows = slice(i * p, (i + 1) * p)
                    out_ref[m, rows, :] = out_ref[m, rows, :] - jnp.dot(
                        col[rows], full, precision=HIGHEST, preferred_element_type=jnp.float32
                    )


def inverses(summed):
    return pl.pallas_call(
        inverse_kernel,
        out_shape=jax.ShapeDtypeStruct((2, F, F), jnp.float32),
        grid=(1,),
        in_specs=[pl.BlockSpec((2 * SLABS * F, LANES), lambda i: (0, 0))],
        out_specs=pl.BlockSpec((2, F, F), lambda i: (0, 0, 0)),
        compiler_params=pltpu.CompilerParams(vmem_limit_bytes=48 * 2**20),
        name="inverses",
    )(summed)


def split(value):
    high = value.astype(jnp.bfloat16)
    return high, (value - high.astype(jnp.float32)).astype(jnp.bfloat16)


def dot(a, b):
    return jnp.dot(a, b, preferred_element_type=jnp.float32)


def sweep_kernel(inv_ref, inv2_ref, g_ref, g2_ref, c_ref, ft_ref, y_ref, coef_ref, res_ref,
                 ih, il, gh, gl):
    core = lax.axis_index("blk")
    for own, (iref, gref) in enumerate(((inv_ref, g_ref), (inv2_ref, g2_ref))):
        owner = core if own == 0 else 1 - core
        for k in range(2):
            high, low = split(iref[k])
            ih[2 * owner + k] = high
            il[2 * owner + k] = low
        for k in range(3):
            for j in range(SLABS):
                high, low = split(gref[pl.ds((k * SLABS + j) * F, F), :])
                cols = slice(j * LANES, (j + 1) * LANES)
                gh[3 * owner + k, :, cols] = high
                gl[3 * owner + k, :, cols] = low
    where = {(1, 0): 0, (2, 0): 1, (3, 1): 2, (3, 2): 3, (2, 1): 4, (3, 0): 5}

    def one(half, _):
        cols = pl.ds(pl.multiple_of(half * 256, 256), 256)
        rounded = []
        for b in range(4):
            corr = jnp.concatenate(
                [
                    c_ref[pl.ds(pl.multiple_of((b * SLABS + 2 * half + k) * F, F), F), :]
                    for k in range(2)
                ],
                axis=1,
            )
            for j in range(b):
                corr = corr - (dot(gh[where[b, j]], rounded[j]) + dot(gl[where[b, j]], rounded[j]))
            ch, cl = split(corr)
            delta = dot(ih[b], ch) + (dot(ih[b], cl) + dot(il[b], ch))
            coef_ref[b, :, cols] = delta
            rounded.append(delta.astype(jnp.bfloat16))
        fit = lax.dot_general(
            ft_ref[0], rounded[0], (((0,), (0,)), ((), ())), preferred_element_type=jnp.float32
        )
        for b in range(1, 4):
            fit = fit + lax.dot_general(
                ft_ref[b], rounded[b], (((0,), (0,)), ((), ())), preferred_element_type=jnp.float32
            )
        res_ref[:, cols] = y_ref[:, cols].astype(jnp.float32) - fit
        return 0

    lax.fori_loop(0, 2, one, 0)


def sweep(inv, inv2, g, g2, c, ft, y):
    vmem = pl.BlockSpec(memory_space=pltpu.VMEM)
    return pl.pallas_call(
        sweep_kernel,
        out_shape=(
            jax.ShapeDtypeStruct((4, F, y.shape[1]), jnp.float32),
            jax.ShapeDtypeStruct(y.shape, jnp.float32),
        ),
        in_specs=[vmem] * 7,
        out_specs=(vmem, vmem),
        scratch_shapes=[
            pltpu.VMEM((4, F, F), jnp.bfloat16),
            pltpu.VMEM((4, F, F), jnp.bfloat16),
            pltpu.VMEM((6, F, F), jnp.bfloat16),
            pltpu.VMEM((6, F, F), jnp.bfloat16),
        ],
        compiler_params=pltpu.CompilerParams(vmem_limit_bytes=62 * 2**20),
        name="sweep",
    )(inv, inv2, g, g2, c, ft, y)


def body(inputs, proj, phase, targets):
    projt = jnp.swapaxes(proj, 1, 2)
    shift = phase.astype(jnp.float32)[:, :, None]
    ft, parts = features_and_parts(inputs, projt, shift, targets)
    summed = ring_sum(parts)
    inv = inverses(summed)
    cross = summed[2 * SLABS * F:5 * SLABS * F]
    moments = summed[5 * SLABS * F:]
    swap = [(0, 1), (1, 0)]
    cross2 = lax.ppermute(cross, "blk", swap)
    inv2 = lax.ppermute(inv, "blk", swap)
    return sweep(inv, inv2, cross, cross2, moments, ft, targets)


def solution(mesh):
    return jax.shard_map(
        body,
        mesh=mesh,
        in_specs=(P("rows", None), P("blk", None, None), P("blk", None), P("rows", "blk")),
        out_specs=(P(None, None, "blk"), P("rows", "blk")),
        check_vma=False,
    )
```

```python
import functools
import math

import jax
import jax.numpy as jnp
from jax import lax
from jax.experimental import pallas as pl
from jax.experimental.pallas import tpu as pltpu
from jax.sharding import PartitionSpec as P

MESH = pl.DeviceIdType.MESH
LOGICAL = pl.DeviceIdType.LOGICAL
HIGHEST = lax.Precision.HIGHEST
ridge = 0.05

F = 512
LANES = 128
SLABS = F // LANES
TILES = SLABS * (SLABS + 1) // 2
CROSS = 2 * TILES * LANES
MOMENT = CROSS + 3 * SLABS * F
DATA_ROWS = MOMENT + 4 * SLABS * F


def tile_row(m, i, j):
    return (m * TILES + i * (i + 1) // 2 + j) * LANES


def sibling():
    return {"blk": 1 - lax.axis_index("blk")}


def cos_turns(t):
    u = jnp.abs(t) - 0.25
    w = u * u
    acc = jnp.full_like(w, SIN_POLY[-1])
    for coef in SIN_POLY[-2::-1]:
        acc = acc * w + coef
    return acc * u


def fit_sin_poly():
    import numpy as np

    degree = 5
    nodes = (np.cos((np.arange(degree + 1) + 0.5) * np.pi / (degree + 1)) + 1.0) / 32.0
    root = np.sqrt(nodes)
    values = -np.sin(2 * np.pi * root) / root
    vander = np.vander(nodes, degree + 1, increasing=True)
    return [float(v) for v in np.linalg.solve(vander, values)]


SIN_POLY = fit_sin_poly()


def feature_kernel(scale, xt_ref, proj_ref, phase_ref, y_ref, ft_ref, part_ref, send_sem, recv_sem):
    core = lax.axis_index("blk")
    rows = xt_ref.shape[1]
    barrier = pltpu.get_barrier_semaphore()
    pl.semaphore_signal(barrier, inc=1, device_id=sibling(), device_id_type=MESH)
    pl.semaphore_wait(barrier, 1)

    chunk = 256
    copies = []
    for i in range(2):
        g = 2 * core + i
        shift = jnp.broadcast_to(phase_ref[i:i + 1, :].astype(jnp.float32), (8, F)).T[:, :1]

        def piece(j, _, i=i, g=g, shift=shift):
            cols = pl.ds(pl.multiple_of(j * chunk, chunk), chunk)
            pre = lax.dot_general(
                proj_ref[i], xt_ref[:, cols], (((0,), (0,)), ((), ())), preferred_element_type=jnp.float32
            )
            turns = (pre + shift) * (0.5 / math.pi)
            turns = turns - jnp.round(turns)
            ft_ref[g, :, cols] = (cos_turns(turns) * scale).astype(jnp.bfloat16)
            return 0

        lax.fori_loop(0, rows // chunk, piece, 0)
        copy = pltpu.make_async_remote_copy(
            src_ref=ft_ref.at[g],
            dst_ref=ft_ref.at[g],
            send_sem=send_sem.at[i],
            recv_sem=recv_sem.at[i],
            device_id=sibling(),
            device_id_type=MESH,
        )
        copy.start()
        copies.append(copy)

    def put(base, half, value):
        for k in range(2):
            row = pl.multiple_of(base + (2 * half + k) * F, LANES)
            part_ref[pl.ds(row, F), :] = value[:, k * LANES:(k + 1) * LANES]

    def diagonal(m, a):
        for half in range(2):
            top = 256 * half
            value = lax.dot_general(
                ft_ref[a, top:, :], ft_ref[a, top:top + 256, :], (((1,), (1,)), ((), ())),
                preferred_element_type=jnp.float32,
            )
            for k in range(2):
                j = 2 * half + k
                for i in range(j, SLABS):
                    rows = slice(i * LANES - top, (i + 1) * LANES - top)
                    part_ref[pl.ds(tile_row(m, i, j), LANES), :] = value[rows, k * LANES:(k + 1) * LANES]

    def gram(q, a, b):
        def one(half, _):
            cols = pl.ds(pl.multiple_of(half * 256, 256), 256)
            put(CROSS + q * SLABS * F, half, lax.dot_general(
                ft_ref[a], ft_ref[b, cols, :], (((1,), (1,)), ((), ())), preferred_element_type=jnp.float32
            ))
            return 0

        lax.fori_loop(0, 2, one, 0)

    def moment(b):
        def one(half, _):
            cols = pl.ds(pl.multiple_of(half * 256, 256), 256)
            put(MOMENT + b * SLABS * F, half, jnp.dot(ft_ref[b], y_ref[:, cols], preferred_element_type=jnp.float32))
            return 0

        lax.fori_loop(0, 2, one, 0)

    own = [2 * core, 2 * core + 1]
    other = [2 * (1 - core), 2 * (1 - core) + 1]
    diagonal(0, own[0])
    diagonal(1, own[1])
    gram(0, own[1], own[0])
    moment(own[0])
    moment(own[1])
    for i in range(2):
        pltpu.make_async_remote_copy(
            src_ref=ft_ref.at[own[i]],
            dst_ref=ft_ref.at[other[i]],
            send_sem=send_sem.at[i],
            recv_sem=recv_sem.at[i],
            device_id=sibling(),
            device_id_type=MESH,
        ).wait_recv()
    gram(1, 2, core)
    gram(2, 3, 1 - core)
    moment(other[0])
    moment(other[1])
    for copy in copies:
        copy.wait_send()


def features_and_parts(xt, proj, phase, y):
    rows = xt.shape[1]
    scale = 1.0 / math.sqrt(rows * 128)
    vmem = pl.BlockSpec(memory_space=pltpu.VMEM)
    return pl.pallas_call(
        functools.partial(feature_kernel, scale),
        out_shape=(
            jax.ShapeDtypeStruct((4, F, rows), jnp.bfloat16),
            jax.ShapeDtypeStruct((DATA_ROWS, LANES), jnp.float32),
        ),
        in_specs=[vmem] * 4,
        out_specs=(vmem, vmem),
        scratch_shapes=[pltpu.SemaphoreType.DMA((2,)), pltpu.SemaphoreType.DMA((2,))],
        compiler_params=pltpu.CompilerParams(
            collective_id=0, has_side_effects=True, vmem_limit_bytes=60 * 2**20
        ),
        name="features",
    )(xt, proj, phase, y)


AXES = ((4, 32), (8, 4), (4, 1))
Y, Z, X = 0, 1, 2
PARTS = (((Y, X, Z), None), ((Z, X), Y), ((X, Y, Z), None))


def coords():
    r = lax.axis_index("rows")
    return r, [lax.rem(r // stride, n) for n, stride in AXES]


class Stream:
    def __init__(self, index, part, direction, base, length, held, modes):
        self.index, self.dir, self.base = index, direction, base
        self.order, last = PARTS[part]
        depth = len(self.order)
        self.rows = []
        for a in self.order:
            length //= AXES[a][0]
            self.rows.append(length)
        assert length % 8 == 0
        scatter = [("rs", a, i, self.rows[i], modes[part][i]) for i, a in enumerate(self.order)]
        middle = [] if last is None else [("ar", last, depth - 1, self.rows[-1], "direct")]
        gather = [("ag", a, i, rows, mode) for _, a, i, rows, mode in scatter[::-1]]
        self.stages = scatter + middle + gather
        self.final = len(scatter + middle) - 1
        self.first, self.slots, count = [], [], 0
        for kind, axis, pos, rows, mode in self.stages:
            n = AXES[axis][0]
            self.first.append(count)
            count += n - 1
            if kind != "ag":
                self.slots.append([held + s * rows for s in range(n - 1)])
                held += (n - 1) * rows
        self.count, self.held_end = count, held
        self.sums = [
            slots[-1 if self.stages[t][4] == "ring" else 0] for t, slots in enumerate(self.slots)
        ]
        self.events = []
        for g, (kind, axis, pos, rows, mode) in enumerate(self.stages):
            n = AXES[axis][0]
            after = self.initial(g + 1)
            if mode == "ring":
                for s in range(n - 1):
                    self.events.append(([(g, s)], (g, s), [(g, s + 1)] if s < n - 2 else after))
            else:
                self.events.append(([(g, s) for s in range(n - 1)], (g, None), after))

    def initial(self, g):
        if g >= len(self.stages):
            return []
        n = AXES[self.stages[g][1]][0]
        return [(g, 0)] if self.stages[g][4] == "ring" else [(g, s) for s in range(n - 1)]


class Plan:
    def __init__(self, rounds, latency=2.4, rate=47e3, extra=()):
        self.streams, held, base = [], 0, 0
        for number, (units, modes, delay) in enumerate(rounds):
            for part in range(3):
                for d in range(2):
                    length = units[part]
                    if not length:
                        continue
                    st = Stream(len(self.streams), part, (1, -1)[d], base, length, held, modes)
                    st.round, st.delay = number, delay
                    held = st.held_end
                    base += length
                    self.streams.append(st)
        self.held, self.rows = held, base
        self.copies = max(st.count for st in self.streams)
        self.simulate(latency, rate, extra)

    def simulate(self, latency, rate, extra=()):
        free, order, ready, core = {}, [], [], 0.0
        arrival = {}

        def send(st, copy, now):
            g, s = copy
            kind, axis, pos, rows, mode = st.stages[g]
            n = AXES[axis][0]
            hops, direction = 1, st.dir
            if mode == "direct":
                hops = min(s + 1, n - s - 1)
                direction = 1 if s + 1 <= n // 2 else -1
            link = (axis, direction)
            start = max(now, free.get(link, 0.0))
            free[link] = start + hops * rows * LANES * 4 / rate
            arrival[st.index, copy] = free[link] + latency + 0.8 * (hops - 1)

        nxt = {}
        for st in self.streams:
            nxt[st.index] = -1
        pieces, done0 = list(extra), len([s for s in self.streams if s.round == 0])
        self.round_end = {}
        while True:
            best = None
            for st in self.streams:
                e = nxt[st.index]
                if e >= len(st.events):
                    continue
                when = st.delay if e < 0 else max(arrival[st.index, c] for c in st.events[e][0])
                key = (max(when, core), st.round, when, st.index)
                if best is None or key < best[0]:
                    best = (key, st)
            if best is None:
                break
            if pieces and done0 == 0 and best[0][0] > core + 0.3:
                core += pieces.pop(0)
                order.append(("piece", None))
                continue
            when, st = best[0][0], best[1]
            e = nxt[st.index]
            core = when + 0.1
            order.append((st.index, e))
            for copy in (st.initial(0) if e < 0 else st.events[e][2]):
                send(st, copy, core)
            nxt[st.index] += 1
            if nxt[st.index] >= len(st.events):
                self.round_end[st.round] = core
                if st.round == 0:
                    done0 -= 1
                order.append(("end", st.index))
        for _ in pieces:
            order.append(("piece", None))
        self.order, self.time = order, core + sum(pieces)


def add_into(dst, dst_off, terms, rows):
    step = rows
    for cand in (192, 144, 128, 96, 72, 64):
        if rows > cand and rows % cand == 0:
            step = cand
            break

    def value(term, j):
        if isinstance(term[0], tuple):
            total = value(term[0], j)
            for other in term[1:]:
                total = total + value(other, j)
            return total
        ref, off = term
        return ref[pl.ds(aligned(off + j * step), step), :]

    def one(j, _):
        dst[pl.ds(aligned(dst_off + j * step), step), :] = value(terms, j)
        return 0

    if step == rows:
        one(0, 0)
    else:
        lax.fori_loop(0, rows // step, one, 0)


def aligned(v):
    return v if isinstance(v, int) else pl.multiple_of(v, 8)


class Ring:
    def __init__(self, plan, data_ref, out_ref, held, send_sem, recv_sem):
        self.plan, self.data, self.out, self.held = plan, data_ref, out_ref, held
        self.send_sem, self.recv_sem = send_sem, recv_sem
        self.r, self.here = coords()
        core = lax.axis_index("blk")
        self.chunks, self.ids, self.bases = {}, {}, {}
        for axis, (n, stride) in enumerate(AXES):
            for offset in range(n):
                k = lax.rem(self.here[axis] + offset, n) if offset else self.here[axis]
                self.chunks[axis, offset] = k
                self.ids[axis, offset] = 2 * (self.r + (k - self.here[axis]) * stride) + core

    def neighbour(self, axis, offset):
        return self.ids[axis, offset % AXES[axis][0]]

    def chunk(self, axis, offset):
        return self.chunks[axis, offset % AXES[axis][0]]

    def own(self, st, g, k):
        if g == 0:
            return self.data, aligned(st.base + k * st.rows[0])
        return self.held, aligned(st.sums[g - 1] + k * st.rows[g])

    def place(self, st, pos, k):
        if (st.index, pos) not in self.bases:
            off = st.base
            for i in range(pos):
                off = off + self.here[st.order[i]] * st.rows[i]
            self.bases[st.index, pos] = off
        return aligned(self.bases[st.index, pos] + k * st.rows[pos])

    def copy(self, st, copy, receive=False):
        g, s = copy
        kind, axis, pos, rows, mode = st.stages[g]
        ring = mode == "ring"
        target = st.dir if ring else s + 1
        if kind == "rs":
            if ring and s > 0:
                src = self.held, st.slots[g][s - 1]
            else:
                src = self.own(st, g, self.chunk(axis, -st.dir if ring else s + 1))
            dst = self.held, st.slots[g][s]
        elif kind == "ar":
            src = self.held, st.sums[g - 1]
            dst = self.held, st.slots[g][s]
        else:
            ahead = -st.dir * s if ring else 0
            back = -st.dir * (s + 1) if ring else -(s + 1)
            src = self.out, self.place(st, pos, self.chunk(axis, ahead))
            dst = self.out, self.place(st, pos, self.chunk(axis, back if receive else ahead))
        return pltpu.make_async_remote_copy(
            src_ref=src[0].at[pl.ds(src[1], rows), :],
            dst_ref=dst[0].at[pl.ds(dst[1], rows), :],
            send_sem=self.send_sem.at[st.index, st.first[g] + s],
            recv_sem=self.recv_sem.at[st.index, st.first[g] + s],
            device_id=self.neighbour(axis, target),
            device_id_type=LOGICAL,
        )

    def event(self, index, e):
        st = self.plan.streams[index]
        if e < 0:
            for c in st.initial(0):
                self.copy(st, c).start()
            return
        waits, (g, s), sends = st.events[e]
        for c in waits:
            self.copy(st, c, receive=True).wait_recv()
        kind, axis, pos, rows, mode = st.stages[g]
        if kind != "ag":
            final = g == st.final and s in (None, AXES[axis][0] - 2)
            if kind == "ar":
                a, b, c = [(self.held, slot) for slot in st.slots[g]]
                terms = (((self.held, st.sums[g - 1]), b), (a, c))
            elif s is None:
                own = self.own(st, g, self.chunk(axis, 0))
                terms = (own,) + tuple((self.held, slot) for slot in st.slots[g])
            else:
                own = self.own(st, g, self.chunk(axis, -st.dir * (s + 2)))
                terms = ((self.held, st.slots[g][s]), own)
            if final:
                dst = self.out, self.place(st, pos, self.chunk(axis if kind == "rs" else st.order[pos], 0))
            else:
                dst = self.held, st.slots[g][s or 0]
            add_into(*dst, terms, rows)
        for c in sends:
            self.copy(st, c).start()

    def finish(self):
        for st in self.plan.streams:
            for g in range(len(st.stages)):
                for s in range(AXES[st.stages[g][1]][0] - 1):
                    self.copy(st, (g, s)).wait_send()

    def devices(self):
        for axis, (n, _) in enumerate(AXES):
            for offset in range(1, n):
                yield self.neighbour(axis, offset)


LOW, HIGH_EIG = 0.05, 130.0
NEWTON = 8


def newton_scales():
    rho = (HIGH_EIG - LOW) / (HIGH_EIG + LOW)
    scales = []
    for _ in range(NEWTON + 1):
        scales.append(2.0 / (2.0 - rho * rho))
        rho = rho * rho / (2.0 - rho * rho)
    return scales


def mm(a, b):
    return jnp.dot(a, b, precision=HIGHEST, preferred_element_type=jnp.float32)


def split(value):
    high = value.astype(jnp.bfloat16)
    return high, (value - high.astype(jnp.float32)).astype(jnp.bfloat16)


class Inverses:
    def __init__(self, src, work, pivot):
        self.src, self.work, self.pivot = src, work, pivot
        self.scales = newton_scales()

    @staticmethod
    def durations():
        return [1.0] + SLABS * ([0.3] + (NEWTON // 2) * [1.4] + [0.8, 0.8])

    def pieces(self):
        yield self.load
        for k in range(SLABS):
            yield functools.partial(self.start, k)
            for i in range(NEWTON // 2):
                yield functools.partial(self.newton, k, i)
            for m in range(2):
                yield functools.partial(self.update, k, m)

    def eye(self):
        shape = (LANES, LANES)
        return lax.broadcasted_iota(jnp.int32, shape, 0) == lax.broadcasted_iota(jnp.int32, shape, 1)

    def load(self):
        eye = jnp.where(self.eye(), jnp.float32(ridge), jnp.float32(0.0))
        for m in range(2):
            for i in range(SLABS):
                for j in range(i + 1):
                    tile = self.src[pl.ds(tile_row(m, i, j), LANES), :]
                    a, b = slice(i * LANES, (i + 1) * LANES), slice(j * LANES, (j + 1) * LANES)
                    if i == j:
                        self.work[m, a, b] = tile + eye
                    else:
                        self.work[m, a, b] = tile
                        self.work[m, b, a] = tile.T

    def start(self, k):
        here = slice(k * LANES, (k + 1) * LANES)
        c, s = 2.0 / (LOW + HIGH_EIG), self.scales[0]
        for m in range(2):
            self.pivot[m] = jnp.where(self.eye(), jnp.float32(2.0 * c * s), jnp.float32(0.0)) - (c * c * s) * self.work[m, here, here]

    def newton(self, k, i):
        here = slice(k * LANES, (k + 1) * LANES)
        first, second = self.scales[1 + 2 * i], self.scales[2 + 2 * i]

        def step(t, _):
            s = jnp.where(t == 0, jnp.float32(first), jnp.float32(second))
            xs = [self.pivot[m] for m in range(2)]
            ax = [mm(self.work[m, here, here], xs[m]) for m in range(2)]
            xax = [mm(xs[m], ax[m]) for m in range(2)]
            for m in range(2):
                self.pivot[m] = s * (2.0 * xs[m] - xax[m])
            return 0

        lax.fori_loop(0, 2, step, 0)

    def update(self, k, m):
        here = slice(k * LANES, (k + 1) * LANES)
        work, inv = self.work, self.pivot[m]
        row = mm(inv, work[m, here, :])
        col = work[m, :, here]
        work[m, :, here] = jnp.zeros_like(col)
        work[m, here, :] = row
        work[m, here, here] = inv
        full = work[m, here, :]
        for i in range(SLABS):
            if i != k:
                rows = slice(i * LANES, (i + 1) * LANES)
                work[m, rows, :] = work[m, rows, :] - mm(col[rows], full)


def sum_kernel(plan, data_ref, out_ref, cross_ref, high_ref, low_ref, held, work, pivot,
               send_sem, recv_sem, pair_send, pair_recv):
    ring = Ring(plan, data_ref, out_ref, held, send_sem, recv_sem)
    core = lax.axis_index("blk")
    other = 2 * ring.r + 1 - core
    barrier = pltpu.get_barrier_semaphore()
    met = 1
    pl.semaphore_signal(barrier, inc=1, device_id=other, device_id_type=LOGICAL)
    for device in ring.devices():
        pl.semaphore_signal(barrier, inc=1, device_id=device, device_id_type=LOGICAL)
        met += 1
    pl.semaphore_wait(barrier, met)

    def pair(slot, src, dst):
        return pltpu.make_async_remote_copy(
            src_ref=src, dst_ref=dst, send_sem=pair_send.at[slot], recv_sem=pair_recv.at[slot],
            device_id=other, device_id_type=LOGICAL,
        )

    def cross(slot):
        start, rows = ((0, SLABS * F), (SLABS * F, 2 * SLABS * F))[slot]
        return pair(slot, out_ref.at[pl.ds(CROSS + start, rows), :], cross_ref.at[pl.ds(start, rows), :])

    inverses = Inverses(out_ref, work, pivot)
    pieces = inverses.pieces()
    left = [sum(st.round == n for st in plan.streams) for n in range(3)]
    for what, arg in plan.order:
        if what == "piece":
            next(pieces)()
        elif what == "end":
            n = plan.streams[arg].round
            left[n] -= 1
            if n < 2 and left[n] == 0:
                cross(n).start()
        else:
            ring.event(what, arg)
    for m in range(2):
        high, low = split(work[m])
        high_ref[2 * core + m] = high
        low_ref[2 * core + m] = low
    for k, ref in enumerate((high_ref, low_ref)):
        pair(2 + k, ref.at[pl.ds(2 * core, 2)], ref.at[pl.ds(2 * core, 2)]).start()
    ring.finish()
    for slot in range(2):
        cross(slot).wait()
    for k, ref in enumerate((high_ref, low_ref)):
        pair(2 + k, ref.at[pl.ds(2 * core, 2)], ref.at[pl.ds(2 * (1 - core), 2)]).wait()


def mode(first, second, middle):
    return ((first, second, "direct"), (middle, second), (first, second, "direct"))


ROUNDS = (
    ((1024, 256, 1024), mode("ring", "direct", "ring"), 0.0),
    ((1024, 1024, 1024), mode("ring", "ring", "ring"), 1.0),
    ((1024, 1024, 1024), mode("ring", "ring", "ring"), 2.0),
)


def sum_and_invert(data):
    plan = Plan(ROUNDS, extra=Inverses.durations())
    assert plan.rows == data.shape[0] == DATA_ROWS
    vmem = pl.BlockSpec(memory_space=pltpu.VMEM)
    sems = pltpu.SemaphoreType.DMA((len(plan.streams), plan.copies))
    return pl.pallas_call(
        functools.partial(sum_kernel, plan),
        out_shape=(
            jax.ShapeDtypeStruct(data.shape, jnp.float32),
            jax.ShapeDtypeStruct((3 * SLABS * F, LANES), jnp.float32),
            jax.ShapeDtypeStruct((4, F, F), jnp.bfloat16),
            jax.ShapeDtypeStruct((4, F, F), jnp.bfloat16),
        ),
        in_specs=[vmem],
        out_specs=(vmem,) * 4,
        scratch_shapes=[
            pltpu.VMEM((plan.held, LANES), jnp.float32),
            pltpu.VMEM((2, F, F), jnp.float32),
            pltpu.VMEM((2, LANES, LANES), jnp.float32),
            sems,
            sems,
            pltpu.SemaphoreType.DMA((4,)),
            pltpu.SemaphoreType.DMA((4,)),
        ],
        compiler_params=pltpu.CompilerParams(
            collective_id=1, has_side_effects=True, vmem_limit_bytes=60 * 2**20
        ),
        name="sum_and_invert",
    )(data)


def dot(a, b):
    return jnp.dot(a, b, preferred_element_type=jnp.float32)


def sweep_kernel(sum_ref, cross_ref, ih, il, ft_ref, y_ref, coef_ref, res_ref, gh, gl):
    core = lax.axis_index("blk")
    for own, (gref, base) in enumerate(((sum_ref, CROSS), (cross_ref, 0))):
        owner = core if own == 0 else 1 - core
        for k in range(3):
            for j in range(SLABS):
                high, low = split(gref[pl.ds(base + (k * SLABS + j) * F, F), :])
                cols = slice(j * LANES, (j + 1) * LANES)
                gh[3 * owner + k, :, cols] = high
                gl[3 * owner + k, :, cols] = low
    where = {(1, 0): 0, (2, 0): 1, (3, 1): 2, (3, 2): 3, (2, 1): 4, (3, 0): 5}

    def one(half, _):
        cols = pl.ds(pl.multiple_of(half * 256, 256), 256)
        rounded = []
        for b in range(4):
            corr = jnp.concatenate(
                [
                    sum_ref[pl.ds(pl.multiple_of(MOMENT + (b * SLABS + 2 * half + k) * F, F), F), :]
                    for k in range(2)
                ],
                axis=1,
            )
            for j in range(b):
                corr = corr - (dot(gh[where[b, j]], rounded[j]) + dot(gl[where[b, j]], rounded[j]))
            ch, cl = split(corr)
            delta = dot(ih[b], ch) + (dot(ih[b], cl) + dot(il[b], ch))
            coef_ref[b, :, cols] = delta
            rounded.append(delta.astype(jnp.bfloat16))
        fit = lax.dot_general(
            ft_ref[0], rounded[0], (((0,), (0,)), ((), ())), preferred_element_type=jnp.float32
        )
        for b in range(1, 4):
            fit = fit + lax.dot_general(
                ft_ref[b], rounded[b], (((0,), (0,)), ((), ())), preferred_element_type=jnp.float32
            )
        res_ref[:, cols] = y_ref[:, cols].astype(jnp.float32) - fit
        return 0

    lax.fori_loop(0, 2, one, 0)


def sweep(summed, cross, high, low, ft, y):
    vmem = pl.BlockSpec(memory_space=pltpu.VMEM)
    return pl.pallas_call(
        sweep_kernel,
        out_shape=(
            jax.ShapeDtypeStruct((4, F, y.shape[1]), jnp.float32),
            jax.ShapeDtypeStruct(y.shape, jnp.float32),
        ),
        in_specs=[vmem] * 6,
        out_specs=(vmem, vmem),
        scratch_shapes=[pltpu.VMEM((6, F, F), jnp.bfloat16), pltpu.VMEM((6, F, F), jnp.bfloat16)],
        compiler_params=pltpu.CompilerParams(vmem_limit_bytes=60 * 2**20),
        name="sweep",
    )(summed, cross, high, low, ft, y)


def body(inputs, proj, phase, targets):
    ft, parts = features_and_parts(jnp.swapaxes(inputs, 0, 1), proj, phase, targets)
    return sweep(*sum_and_invert(parts), ft, targets)


def solution(mesh):
    return jax.shard_map(
        body,
        mesh=mesh,
        in_specs=(P("rows", None), P("blk", None, None), P("blk", None), P("rows", "blk")),
        out_specs=(P(None, None, "blk"), P("rows", "blk")),
        check_vma=False,
    )
```

```python
import functools
import math

import jax
import jax.numpy as jnp
from jax import lax
from jax.experimental import pallas as pl
from jax.experimental.pallas import tpu as pltpu
from jax.sharding import PartitionSpec as P

MESH = pl.DeviceIdType.MESH
LOGICAL = pl.DeviceIdType.LOGICAL
HIGHEST = lax.Precision.HIGHEST
ridge = 0.05

F = 512
LANES = 128
SLABS = F // LANES
TILES = SLABS * (SLABS + 1) // 2
CROSS = 2 * TILES * LANES
MOMENT = CROSS + 3 * SLABS * F
DATA_ROWS = MOMENT + 4 * SLABS * F


def tile_row(m, i, j):
    return (m * TILES + i * (i + 1) // 2 + j) * LANES


def sibling():
    return {"blk": 1 - lax.axis_index("blk")}


def cos_turns(t):
    u = jnp.abs(t) - 0.25
    w = u * u
    acc = jnp.full_like(w, SIN_POLY[-1])
    for coef in SIN_POLY[-2::-1]:
        acc = acc * w + coef
    return acc * u


def fit_sin_poly():
    import numpy as np

    degree = 5
    nodes = (np.cos((np.arange(degree + 1) + 0.5) * np.pi / (degree + 1)) + 1.0) / 32.0
    root = np.sqrt(nodes)
    values = -np.sin(2 * np.pi * root) / root
    vander = np.vander(nodes, degree + 1, increasing=True)
    return [float(v) for v in np.linalg.solve(vander, values)]


SIN_POLY = fit_sin_poly()


class Parts:
    def __init__(self, scale, xt_ref, proj_ref, phase_ref, y_ref, ft_ref, part_ref, send_sem, recv_sem):
        self.scale, self.xt, self.proj, self.phase, self.y = scale, xt_ref, proj_ref, phase_ref, y_ref
        self.ft, self.part, self.send_sem, self.recv_sem = ft_ref, part_ref, send_sem, recv_sem
        self.core = lax.axis_index("blk")
        self.own = [2 * self.core, 2 * self.core + 1]
        self.other = [2 * (1 - self.core), 2 * (1 - self.core) + 1]

    def exchange(self, i, receive=False):
        return pltpu.make_async_remote_copy(
            src_ref=self.ft.at[self.own[i]],
            dst_ref=self.ft.at[(self.other if receive else self.own)[i]],
            send_sem=self.send_sem.at[i],
            recv_sem=self.recv_sem.at[i],
            device_id=sibling(),
            device_id_type=MESH,
        )

    def features(self, i):
        chunk = 256
        shift = jnp.broadcast_to(self.phase[i:i + 1, :].astype(jnp.float32), (8, F)).T[:, :1]

        def piece(j, _):
            cols = pl.ds(pl.multiple_of(j * chunk, chunk), chunk)
            pre = lax.dot_general(
                self.proj[i], self.xt[:, cols], (((0,), (0,)), ((), ())), preferred_element_type=jnp.float32
            )
            turns = (pre + shift) * (0.5 / math.pi)
            turns = turns - jnp.round(turns)
            self.ft[self.own[i], :, cols] = (cos_turns(turns) * self.scale).astype(jnp.bfloat16)
            return 0

        lax.fori_loop(0, self.xt.shape[1] // chunk, piece, 0)
        self.exchange(i).start()

    def put(self, base, half, value):
        for k in range(2):
            row = pl.multiple_of(base + (2 * half + k) * F, LANES)
            self.part[pl.ds(row, F), :] = value[:, k * LANES:(k + 1) * LANES]

    def diagonal(self, m):
        a = self.own[m]
        for half in range(2):
            top = 256 * half
            value = lax.dot_general(
                self.ft[a, top:, :], self.ft[a, top:top + 256, :], (((1,), (1,)), ((), ())),
                preferred_element_type=jnp.float32,
            )
            for k in range(2):
                j = 2 * half + k
                for i in range(j, SLABS):
                    rows = slice(i * LANES - top, (i + 1) * LANES - top)
                    self.part[pl.ds(tile_row(m, i, j), LANES), :] = value[rows, k * LANES:(k + 1) * LANES]

    def gram(self, q, a, b):
        def one(half, _):
            cols = pl.ds(pl.multiple_of(half * 256, 256), 256)
            self.put(CROSS + q * SLABS * F, half, lax.dot_general(
                self.ft[a], self.ft[b, cols, :], (((1,), (1,)), ((), ())), preferred_element_type=jnp.float32
            ))
            return 0

        lax.fori_loop(0, 2, one, 0)

    def moment(self, b):
        def one(half, _):
            cols = pl.ds(pl.multiple_of(half * 256, 256), 256)
            self.put(MOMENT + b * SLABS * F, half, jnp.dot(
                self.ft[b], self.y[:, cols], preferred_element_type=jnp.float32
            ))
            return 0

        lax.fori_loop(0, 2, one, 0)

    def first(self):
        for i in range(2):
            self.features(i)
        for i in range(2):
            self.diagonal(i)
        self.gram(0, self.own[1], self.own[0])

    @staticmethod
    def durations():
        return [1.0] * 6

    def rest(self):
        yield functools.partial(self.moment, self.own[0])
        yield functools.partial(self.moment, self.own[1])

        def crossed():
            for i in range(2):
                self.exchange(i, receive=True).wait_recv()
            self.gram(1, 2, self.core)

        yield crossed
        yield functools.partial(self.gram, 2, 3, 1 - self.core)
        yield functools.partial(self.moment, self.other[0])
        yield functools.partial(self.moment, self.other[1])

    def finish(self):
        for i in range(2):
            self.exchange(i).wait_send()


AXES = ((4, 32), (8, 4), (4, 1))
Y, Z, X = 0, 1, 2
PARTS = (((Y, X, Z), None), ((Z, X), Y), ((X, Y, Z), None))


def coords():
    r = lax.axis_index("rows")
    return r, [lax.rem(r // stride, n) for n, stride in AXES]


class Stream:
    def __init__(self, index, part, direction, base, length, held, modes):
        self.index, self.dir, self.base = index, direction, base
        self.order, last = PARTS[part]
        depth = len(self.order)
        self.rows = []
        for a in self.order:
            length //= AXES[a][0]
            self.rows.append(length)
        assert length % 8 == 0
        scatter = [("rs", a, i, self.rows[i], modes[part][i]) for i, a in enumerate(self.order)]
        middle = [] if last is None else [("ar", last, depth - 1, self.rows[-1], "direct")]
        gather = [("ag", a, i, rows, mode) for _, a, i, rows, mode in scatter[::-1]]
        self.stages = scatter + middle + gather
        self.final = len(scatter + middle) - 1
        self.first, self.slots, count = [], [], 0
        for kind, axis, pos, rows, mode in self.stages:
            n = AXES[axis][0]
            self.first.append(count)
            count += n - 1
            if kind != "ag":
                self.slots.append([held + s * rows for s in range(n - 1)])
                held += (n - 1) * rows
        self.count, self.held_end = count, held
        self.sums = [
            slots[-1 if self.stages[t][4] == "ring" else 0] for t, slots in enumerate(self.slots)
        ]
        self.events = []
        for g, (kind, axis, pos, rows, mode) in enumerate(self.stages):
            n = AXES[axis][0]
            after = self.initial(g + 1)
            if mode == "ring":
                for s in range(n - 1):
                    self.events.append(([(g, s)], (g, s), [(g, s + 1)] if s < n - 2 else after))
            else:
                self.events.append(([(g, s) for s in range(n - 1)], (g, None), after))

    def initial(self, g):
        if g >= len(self.stages):
            return []
        n = AXES[self.stages[g][1]][0]
        return [(g, 0)] if self.stages[g][4] == "ring" else [(g, s) for s in range(n - 1)]


class Plan:
    def __init__(self, rounds, latency=2.0, rate=47e3, extra=(), before=()):
        self.streams, held, base = [], 0, 0
        for number, (units, modes, delay) in enumerate(rounds):
            for part in range(3):
                for d in range(2):
                    length = units[part]
                    if not length:
                        continue
                    st = Stream(len(self.streams), part, (1, -1)[d], base, length, held, modes)
                    st.round, st.delay = number, delay
                    held = st.held_end
                    base += length
                    self.streams.append(st)
        self.held, self.rows = held, base
        self.copies = max(st.count for st in self.streams)
        self.simulate(latency, rate, extra, before)

    def simulate(self, latency, rate, extra=(), before=()):
        free, order, ready, core = {}, [], [], 0.0
        arrival = {}

        def send(st, copy, now):
            g, s = copy
            kind, axis, pos, rows, mode = st.stages[g]
            n = AXES[axis][0]
            hops, direction = 1, st.dir
            if mode == "direct":
                hops = min(s + 1, n - s - 1)
                direction = 1 if s + 1 <= n // 2 else -1
            link = (axis, direction)
            start = max(now, free.get(link, 0.0))
            free[link] = start + hops * rows * LANES * 4 / rate
            arrival[st.index, copy] = free[link] + latency + 0.8 * (hops - 1)

        nxt = {}
        for st in self.streams:
            nxt[st.index] = -1
        early = list(before)
        pieces, done0 = list(extra), len([s for s in self.streams if s.round == 0])
        self.round_end = {}
        while True:
            best = None
            for st in self.streams:
                e = nxt[st.index]
                if e >= len(st.events):
                    continue
                when = st.delay if e < 0 else max(arrival[st.index, c] for c in st.events[e][0])
                key = (max(when, core), st.round, when, st.index)
                if best is None or key < best[0]:
                    best = (key, st)
            if best is None:
                break
            if early and (best[0][0] > core + 0.3 or best[1].round > 0):
                core += early.pop(0)
                order.append(("early", None))
                continue
            if pieces and done0 == 0 and best[0][0] > core + 0.3:
                core += pieces.pop(0)
                order.append(("piece", None))
                continue
            when, st = best[0][0], best[1]
            e = nxt[st.index]
            core = when + 0.1
            order.append((st.index, e))
            for copy in (st.initial(0) if e < 0 else st.events[e][2]):
                send(st, copy, core)
            nxt[st.index] += 1
            if nxt[st.index] >= len(st.events):
                self.round_end[st.round] = core
                if st.round == 0:
                    done0 -= 1
                order.append(("end", st.index))
        for _ in pieces:
            order.append(("piece", None))
        self.order, self.time = order, core + sum(pieces)


def add_into(dst, dst_off, terms, rows):
    step = rows
    for cand in (192, 144, 128, 96, 72, 64):
        if rows > cand and rows % cand == 0:
            step = cand
            break

    def value(term, j):
        if isinstance(term[0], tuple):
            total = value(term[0], j)
            for other in term[1:]:
                total = total + value(other, j)
            return total
        ref, off = term
        return ref[pl.ds(aligned(off + j * step), step), :]

    def one(j, _):
        dst[pl.ds(aligned(dst_off + j * step), step), :] = value(terms, j)
        return 0

    if step == rows:
        one(0, 0)
    else:
        lax.fori_loop(0, rows // step, one, 0)


def aligned(v):
    return v if isinstance(v, int) else pl.multiple_of(v, 8)


class Ring:
    def __init__(self, plan, data_ref, out_ref, held, send_sem, recv_sem):
        self.plan, self.data, self.out, self.held = plan, data_ref, out_ref, held
        self.send_sem, self.recv_sem = send_sem, recv_sem
        self.r, self.here = coords()
        core = lax.axis_index("blk")
        self.chunks, self.ids, self.bases = {}, {}, {}
        for axis, (n, stride) in enumerate(AXES):
            for offset in range(n):
                k = lax.rem(self.here[axis] + offset, n) if offset else self.here[axis]
                self.chunks[axis, offset] = k
                self.ids[axis, offset] = 2 * (self.r + (k - self.here[axis]) * stride) + core

    def neighbour(self, axis, offset):
        return self.ids[axis, offset % AXES[axis][0]]

    def chunk(self, axis, offset):
        return self.chunks[axis, offset % AXES[axis][0]]

    def own(self, st, g, k):
        if g == 0:
            return self.data, aligned(st.base + k * st.rows[0])
        return self.held, aligned(st.sums[g - 1] + k * st.rows[g])

    def place(self, st, pos, k):
        if (st.index, pos) not in self.bases:
            off = st.base
            for i in range(pos):
                off = off + self.here[st.order[i]] * st.rows[i]
            self.bases[st.index, pos] = off
        return aligned(self.bases[st.index, pos] + k * st.rows[pos])

    def copy(self, st, copy, receive=False):
        g, s = copy
        kind, axis, pos, rows, mode = st.stages[g]
        ring = mode == "ring"
        target = st.dir if ring else s + 1
        if kind == "rs":
            if ring and s > 0:
                src = self.held, st.slots[g][s - 1]
            else:
                src = self.own(st, g, self.chunk(axis, -st.dir if ring else s + 1))
            dst = self.held, st.slots[g][s]
        elif kind == "ar":
            src = self.held, st.sums[g - 1]
            dst = self.held, st.slots[g][s]
        else:
            ahead = -st.dir * s if ring else 0
            back = -st.dir * (s + 1) if ring else -(s + 1)
            src = self.out, self.place(st, pos, self.chunk(axis, ahead))
            dst = self.out, self.place(st, pos, self.chunk(axis, back if receive else ahead))
        return pltpu.make_async_remote_copy(
            src_ref=src[0].at[pl.ds(src[1], rows), :],
            dst_ref=dst[0].at[pl.ds(dst[1], rows), :],
            send_sem=self.send_sem.at[st.index, st.first[g] + s],
            recv_sem=self.recv_sem.at[st.index, st.first[g] + s],
            device_id=self.neighbour(axis, target),
            device_id_type=LOGICAL,
        )

    def event(self, index, e):
        st = self.plan.streams[index]
        if e < 0:
            for c in st.initial(0):
                self.copy(st, c).start()
            return
        waits, (g, s), sends = st.events[e]
        for c in waits:
            self.copy(st, c, receive=True).wait_recv()
        kind, axis, pos, rows, mode = st.stages[g]
        if kind != "ag":
            final = g == st.final and s in (None, AXES[axis][0] - 2)
            if kind == "ar":
                a, b, c = [(self.held, slot) for slot in st.slots[g]]
                terms = (((self.held, st.sums[g - 1]), b), (a, c))
            elif s is None:
                own = self.own(st, g, self.chunk(axis, 0))
                terms = (own,) + tuple((self.held, slot) for slot in st.slots[g])
            else:
                own = self.own(st, g, self.chunk(axis, -st.dir * (s + 2)))
                terms = ((self.held, st.slots[g][s]), own)
            if final:
                dst = self.out, self.place(st, pos, self.chunk(axis if kind == "rs" else st.order[pos], 0))
            else:
                dst = self.held, st.slots[g][s or 0]
            add_into(*dst, terms, rows)
        for c in sends:
            self.copy(st, c).start()

    def finish(self):
        for st in self.plan.streams:
            for g in range(len(st.stages)):
                for s in range(AXES[st.stages[g][1]][0] - 1):
                    self.copy(st, (g, s)).wait_send()

    def devices(self):
        for axis, (n, _) in enumerate(AXES):
            for offset in range(1, n):
                yield self.neighbour(axis, offset)


LOW, HIGH_EIG = 0.05, 130.0
NEWTON = 8


def newton_scales():
    rho = (HIGH_EIG - LOW) / (HIGH_EIG + LOW)
    scales = []
    for _ in range(NEWTON + 1):
        scales.append(2.0 / (2.0 - rho * rho))
        rho = rho * rho / (2.0 - rho * rho)
    return scales


def mm(a, b):
    return jnp.dot(a, b, precision=HIGHEST, preferred_element_type=jnp.float32)


def split(value):
    high = value.astype(jnp.bfloat16)
    return high, (value - high.astype(jnp.float32)).astype(jnp.bfloat16)


class Inverses:
    def __init__(self, src, work, pivot):
        self.src, self.work, self.pivot = src, work, pivot
        self.scales = newton_scales()

    @staticmethod
    def durations():
        return [1.0] + SLABS * ([0.3] + (NEWTON // 2) * [1.4] + [0.8, 0.8])

    def pieces(self):
        yield self.load
        for k in range(SLABS):
            yield functools.partial(self.start, k)
            for i in range(NEWTON // 2):
                yield functools.partial(self.newton, k, i)
            for m in range(2):
                yield functools.partial(self.update, k, m)

    def eye(self):
        shape = (LANES, LANES)
        return lax.broadcasted_iota(jnp.int32, shape, 0) == lax.broadcasted_iota(jnp.int32, shape, 1)

    def load(self):
        eye = jnp.where(self.eye(), jnp.float32(ridge), jnp.float32(0.0))
        for m in range(2):
            for i in range(SLABS):
                for j in range(i + 1):
                    tile = self.src[pl.ds(tile_row(m, i, j), LANES), :]
                    a, b = slice(i * LANES, (i + 1) * LANES), slice(j * LANES, (j + 1) * LANES)
                    if i == j:
                        self.work[m, a, b] = tile + eye
                    else:
                        self.work[m, a, b] = tile
                        self.work[m, b, a] = tile.T

    def start(self, k):
        here = slice(k * LANES, (k + 1) * LANES)
        c, s = 2.0 / (LOW + HIGH_EIG), self.scales[0]
        for m in range(2):
            self.pivot[m] = jnp.where(self.eye(), jnp.float32(2.0 * c * s), jnp.float32(0.0)) - (c * c * s) * self.work[m, here, here]

    def newton(self, k, i):
        here = slice(k * LANES, (k + 1) * LANES)
        first, second = self.scales[1 + 2 * i], self.scales[2 + 2 * i]

        def step(t, _):
            s = jnp.where(t == 0, jnp.float32(first), jnp.float32(second))
            xs = [self.pivot[m] for m in range(2)]
            ax = [mm(self.work[m, here, here], xs[m]) for m in range(2)]
            xax = [mm(xs[m], ax[m]) for m in range(2)]
            for m in range(2):
                self.pivot[m] = s * (2.0 * xs[m] - xax[m])
            return 0

        lax.fori_loop(0, 2, step, 0)

    def update(self, k, m):
        here = slice(k * LANES, (k + 1) * LANES)
        work, inv = self.work, self.pivot[m]
        row = mm(inv, work[m, here, :])
        col = work[m, :, here]
        work[m, :, here] = jnp.zeros_like(col)
        work[m, here, :] = row
        work[m, here, here] = inv
        full = work[m, here, :]
        for i in range(SLABS):
            if i != k:
                rows = slice(i * LANES, (i + 1) * LANES)
                work[m, rows, :] = work[m, rows, :] - mm(col[rows], full)


def sum_kernel(plan, scale, xt_ref, proj_ref, phase_ref, y_ref, ft_ref, out_ref, cross_ref, high_ref, low_ref,
               data_ref, held, work, pivot, send_sem, recv_sem, pair_send, pair_recv, feat_send, feat_recv):
    ring = Ring(plan, data_ref, out_ref, held, send_sem, recv_sem)
    core = lax.axis_index("blk")
    other = 2 * ring.r + 1 - core
    barrier = pltpu.get_barrier_semaphore()
    met = 1
    pl.semaphore_signal(barrier, inc=1, device_id=other, device_id_type=LOGICAL)
    for device in ring.devices():
        pl.semaphore_signal(barrier, inc=1, device_id=device, device_id_type=LOGICAL)
        met += 1
    pl.semaphore_wait(barrier, met)

    def pair(slot, src, dst):
        return pltpu.make_async_remote_copy(
            src_ref=src, dst_ref=dst, send_sem=pair_send.at[slot], recv_sem=pair_recv.at[slot],
            device_id=other, device_id_type=LOGICAL,
        )

    def cross(slot):
        start, rows = ((0, SLABS * F), (SLABS * F, 2 * SLABS * F))[slot]
        return pair(slot, out_ref.at[pl.ds(CROSS + start, rows), :], cross_ref.at[pl.ds(start, rows), :])

    parts = Parts(scale, xt_ref, proj_ref, phase_ref, y_ref, ft_ref, data_ref, feat_send, feat_recv)
    parts.first()
    early = parts.rest()
    inverses = Inverses(out_ref, work, pivot)
    pieces = inverses.pieces()
    left = [sum(st.round == n for st in plan.streams) for n in range(2)]
    for what, arg in plan.order:
        if what == "piece":
            next(pieces)()
        elif what == "early":
            next(early)()
        elif what == "end":
            n = plan.streams[arg].round
            left[n] -= 1
            if left[n] == 0:
                cross(n).start()
        else:
            ring.event(what, arg)
    for m in range(2):
        high, low = split(work[m])
        high_ref[2 * core + m] = high
        low_ref[2 * core + m] = low
    for k, ref in enumerate((high_ref, low_ref)):
        pair(2 + k, ref.at[pl.ds(2 * core, 2)], ref.at[pl.ds(2 * core, 2)]).start()
    ring.finish()
    parts.finish()
    for slot in range(2):
        cross(slot).wait()
    for k, ref in enumerate((high_ref, low_ref)):
        pair(2 + k, ref.at[pl.ds(2 * core, 2)], ref.at[pl.ds(2 * (1 - core), 2)]).wait()


def mode(first, second, middle):
    return ((first, second, "direct"), (middle, "direct"), (first, second, "direct"))


ROUNDS = (
    ((1024, 256, 1024), mode("ring", "direct", "ring"), 0.0),
    ((2048, 2048, 2048), mode("ring", "ring", "ring"), 7.0),
)


def sum_and_invert(xt, proj, phase, y):
    rows = xt.shape[1]
    scale = 1.0 / math.sqrt(rows * 128)
    plan = Plan(ROUNDS, extra=Inverses.durations(), before=Parts.durations())
    assert plan.rows == DATA_ROWS
    vmem = pl.BlockSpec(memory_space=pltpu.VMEM)
    sems = pltpu.SemaphoreType.DMA((len(plan.streams), plan.copies))
    return pl.pallas_call(
        functools.partial(sum_kernel, plan, scale),
        out_shape=(
            jax.ShapeDtypeStruct((4, F, rows), jnp.bfloat16),
            jax.ShapeDtypeStruct((DATA_ROWS, LANES), jnp.float32),
            jax.ShapeDtypeStruct((3 * SLABS * F, LANES), jnp.float32),
            jax.ShapeDtypeStruct((4, F, F), jnp.bfloat16),
            jax.ShapeDtypeStruct((4, F, F), jnp.bfloat16),
        ),
        in_specs=[vmem] * 4,
        out_specs=(vmem,) * 5,
        scratch_shapes=[
            pltpu.VMEM((DATA_ROWS, LANES), jnp.float32),
            pltpu.VMEM((plan.held, LANES), jnp.float32),
            pltpu.VMEM((2, F, F), jnp.float32),
            pltpu.VMEM((2, LANES, LANES), jnp.float32),
            sems,
            sems,
            pltpu.SemaphoreType.DMA((4,)),
            pltpu.SemaphoreType.DMA((4,)),
            pltpu.SemaphoreType.DMA((2,)),
            pltpu.SemaphoreType.DMA((2,)),
        ],
        compiler_params=pltpu.CompilerParams(
            collective_id=1, has_side_effects=True, vmem_limit_bytes=60 * 2**20
        ),
        name="sum_and_invert",
    )(xt, proj, phase, y)


def dot(a, b):
    return jnp.dot(a, b, preferred_element_type=jnp.float32)


def sweep_kernel(sum_hbm, cross_hbm, ih_hbm, il_hbm, ft_hbm, y_ref, coef_ref, res_ref,
                 own_g, other_g, moments, ih, il, ft, gh, gl, sems):
    core = lax.axis_index("blk")
    half = pl.program_id(0)
    block = SLABS * F
    loads = {}

    def load(name, src, dst):
        loads[name] = pltpu.make_async_copy(src, dst, sems.at[len(loads)])

    for b in range(4):
        load(("high", b), ih_hbm.at[b], ih.at[b])
        load(("low", b), il_hbm.at[b], il.at[b])
        rows = pl.ds(b * block, block)
        load(("moment", b), sum_hbm.at[pl.ds(MOMENT + b * block, block), :], moments.at[rows, :])
        if b == 0:
            load(("own", 0), sum_hbm.at[pl.ds(CROSS, 3 * block), :], own_g)
            load(("other", 0), cross_hbm, other_g)
    for b in range(4):
        load(("ft", b), ft_hbm.at[b], ft.at[b])

    def wait(*names):
        @pl.when(half == 0)
        def _():
            for name in names:
                loads[name].wait()

    @pl.when(half == 0)
    def _():
        for copy in loads.values():
            copy.start()

    where = {(1, 0): 0, (2, 0): 1, (3, 1): 2, (3, 2): 3, (2, 1): 4, (3, 0): 5}
    rounded = []
    for b in range(4):
        wait(("high", b), ("low", b), ("moment", b))
        if b == 1:
            wait(("own", 0), ("other", 0))

            @pl.when(half == 0)
            def _():
                for gref, owner in ((own_g, core), (other_g, 1 - core)):
                    for k in range(3):
                        for j in range(SLABS):
                            high, low = split(gref[pl.ds((k * SLABS + j) * F, F), :])
                            cols = slice(j * LANES, (j + 1) * LANES)
                            gh[3 * owner + k, :, cols] = high
                            gl[3 * owner + k, :, cols] = low

        corr = jnp.concatenate(
            [
                moments[pl.ds(pl.multiple_of((b * SLABS + 2 * half + k) * F, F), F), :]
                for k in range(2)
            ],
            axis=1,
        )
        for j in range(b):
            corr = corr - (dot(gh[where[b, j]], rounded[j]) + dot(gl[where[b, j]], rounded[j]))
        ch, cl = split(corr)
        delta = dot(ih[b], ch) + (dot(ih[b], cl) + dot(il[b], ch))
        coef_ref[b] = delta
        rounded.append(delta.astype(jnp.bfloat16))
    fit = None
    for b in range(4):
        wait(("ft", b))
        term = lax.dot_general(
            ft[b], rounded[b], (((0,), (0,)), ((), ())), preferred_element_type=jnp.float32
        )
        fit = term if fit is None else fit + term
    res_ref[...] = y_ref[...].astype(jnp.float32) - fit


def sweep(ft, summed, cross, high, low, y):
    rows, cols = y.shape
    any_space = pl.BlockSpec(memory_space=pl.ANY)
    return pl.pallas_call(
        sweep_kernel,
        grid=(2,),
        out_shape=(
            jax.ShapeDtypeStruct((4, F, cols), jnp.float32),
            jax.ShapeDtypeStruct(y.shape, jnp.float32),
        ),
        in_specs=[any_space] * 5 + [pl.BlockSpec((rows, cols // 2), lambda i: (0, i))],
        out_specs=(
            pl.BlockSpec((4, F, cols // 2), lambda i: (0, 0, i)),
            pl.BlockSpec((rows, cols // 2), lambda i: (0, i)),
        ),
        scratch_shapes=[
            pltpu.VMEM((3 * SLABS * F, LANES), jnp.float32),
            pltpu.VMEM((3 * SLABS * F, LANES), jnp.float32),
            pltpu.VMEM((4 * SLABS * F, LANES), jnp.float32),
            pltpu.VMEM((4, F, F), jnp.bfloat16),
            pltpu.VMEM((4, F, F), jnp.bfloat16),
            pltpu.VMEM((4, F, rows), jnp.bfloat16),
            pltpu.VMEM((6, F, F), jnp.bfloat16),
            pltpu.VMEM((6, F, F), jnp.bfloat16),
            pltpu.SemaphoreType.DMA((18,)),
        ],
        compiler_params=pltpu.CompilerParams(vmem_limit_bytes=60 * 2**20),
        name="sweep",
    )(summed, cross, high, low, ft, y)


def body(inputs, proj, phase, targets):
    ft, summed, cross, high, low = sum_and_invert(jnp.swapaxes(inputs, 0, 1), proj, phase, targets)
    return sweep(ft, summed, cross, high, low, targets)


def solution(mesh):
    return jax.shard_map(
        body,
        mesh=mesh,
        in_specs=(P("rows", None), P("blk", None, None), P("blk", None), P("rows", "blk")),
        out_specs=(P(None, None, "blk"), P("rows", "blk")),
        check_vma=False,
    )
```

```python
import functools
import math

import jax
import jax.numpy as jnp
from jax import lax
from jax.experimental import pallas as pl
from jax.experimental.pallas import tpu as pltpu
from jax.sharding import PartitionSpec as P

MESH = pl.DeviceIdType.MESH
LOGICAL = pl.DeviceIdType.LOGICAL
HIGHEST = lax.Precision.HIGHEST
ridge = 0.05

F = 512
LANES = 128
SLABS = F // LANES
TILES = SLABS * (SLABS + 1) // 2
CROSS = 2 * TILES * LANES
MOMENT = CROSS + 3 * SLABS * F
DATA_ROWS = MOMENT + 4 * SLABS * F


def tile_row(m, i, j):
    return (m * TILES + i * (i + 1) // 2 + j) * LANES


def sibling():
    return {"blk": 1 - lax.axis_index("blk")}


def cos_turns(t):
    u = jnp.abs(t) - 0.25
    w = u * u
    acc = jnp.full_like(w, SIN_POLY[-1])
    for coef in SIN_POLY[-2::-1]:
        acc = acc * w + coef
    return acc * u


def fit_sin_poly():
    import numpy as np

    degree = 5
    nodes = (np.cos((np.arange(degree + 1) + 0.5) * np.pi / (degree + 1)) + 1.0) / 32.0
    root = np.sqrt(nodes)
    values = -np.sin(2 * np.pi * root) / root
    vander = np.vander(nodes, degree + 1, increasing=True)
    return [float(v) for v in np.linalg.solve(vander, values)]


SIN_POLY = fit_sin_poly()


class Parts:
    def __init__(self, scale, xt_ref, proj_ref, phase_ref, y_ref, ft_ref, part_ref, send_sem, recv_sem):
        self.scale, self.xt, self.proj, self.phase, self.y = scale, xt_ref, proj_ref, phase_ref, y_ref
        self.ft, self.part, self.send_sem, self.recv_sem = ft_ref, part_ref, send_sem, recv_sem
        self.core = lax.axis_index("blk")
        self.own = [2 * self.core, 2 * self.core + 1]
        self.other = [2 * (1 - self.core), 2 * (1 - self.core) + 1]

    def exchange(self, i, receive=False):
        return pltpu.make_async_remote_copy(
            src_ref=self.ft.at[self.own[i]],
            dst_ref=self.ft.at[(self.other if receive else self.own)[i]],
            send_sem=self.send_sem.at[i],
            recv_sem=self.recv_sem.at[i],
            device_id=sibling(),
            device_id_type=MESH,
        )

    def features(self, i):
        chunk = 256
        shift = jnp.broadcast_to(self.phase[i:i + 1, :].astype(jnp.float32), (8, F)).T[:, :1]

        def piece(j, _):
            cols = pl.ds(pl.multiple_of(j * chunk, chunk), chunk)
            pre = lax.dot_general(
                self.proj[i], self.xt[:, cols], (((0,), (0,)), ((), ())), preferred_element_type=jnp.float32
            )
            turns = (pre + shift) * (0.5 / math.pi)
            turns = turns - jnp.round(turns)
            self.ft[self.own[i], :, cols] = (cos_turns(turns) * self.scale).astype(jnp.bfloat16)
            return 0

        lax.fori_loop(0, self.xt.shape[1] // chunk, piece, 0)
        self.exchange(i).start()

    def put(self, base, half, value):
        for k in range(2):
            row = pl.multiple_of(base + (2 * half + k) * F, LANES)
            self.part[pl.ds(row, F), :] = value[:, k * LANES:(k + 1) * LANES]

    def diagonal(self, m):
        a = self.own[m]
        for half in range(2):
            top = 256 * half
            value = lax.dot_general(
                self.ft[a, top:, :], self.ft[a, top:top + 256, :], (((1,), (1,)), ((), ())),
                preferred_element_type=jnp.float32,
            )
            for k in range(2):
                j = 2 * half + k
                for i in range(j, SLABS):
                    rows = slice(i * LANES - top, (i + 1) * LANES - top)
                    self.part[pl.ds(tile_row(m, i, j), LANES), :] = value[rows, k * LANES:(k + 1) * LANES]

    def gram(self, q, a, b):
        def one(half, _):
            cols = pl.ds(pl.multiple_of(half * 256, 256), 256)
            self.put(CROSS + q * SLABS * F, half, lax.dot_general(
                self.ft[a], self.ft[b, cols, :], (((1,), (1,)), ((), ())), preferred_element_type=jnp.float32
            ))
            return 0

        lax.fori_loop(0, 2, one, 0)

    def moment(self, b):
        def one(half, _):
            cols = pl.ds(pl.multiple_of(half * 256, 256), 256)
            self.put(MOMENT + b * SLABS * F, half, jnp.dot(
                self.ft[b], self.y[:, cols], preferred_element_type=jnp.float32
            ))
            return 0

        lax.fori_loop(0, 2, one, 0)

    def first(self):
        for i in range(2):
            self.features(i)
        for i in range(2):
            self.diagonal(i)
        self.gram(0, self.own[1], self.own[0])

    @staticmethod
    def durations():
        return [1.0] * 6

    def rest(self):
        yield functools.partial(self.moment, self.own[0])
        yield functools.partial(self.moment, self.own[1])

        def crossed():
            for i in range(2):
                self.exchange(i, receive=True).wait_recv()
            self.gram(1, 2, self.core)

        yield crossed
        yield functools.partial(self.gram, 2, 3, 1 - self.core)
        yield functools.partial(self.moment, self.other[0])
        yield functools.partial(self.moment, self.other[1])

    def finish(self):
        for i in range(2):
            self.exchange(i).wait_send()


AXES = ((4, 32), (8, 4), (4, 1))
Y, Z, X = 0, 1, 2
PARTS = (((Y, X, Z), None), ((Z, X), Y), ((X, Y, Z), None))


def coords():
    r = lax.axis_index("rows")
    return r, [lax.rem(r // stride, n) for n, stride in AXES]


class Stream:
    def __init__(self, index, part, direction, base, length, held, modes):
        self.index, self.dir, self.base, self.length = index, direction, base, length
        self.order, last = PARTS[part]
        depth = len(self.order)
        self.rows = []
        for a in self.order:
            length //= AXES[a][0]
            self.rows.append(length)
        assert length % 8 == 0
        scatter = [("rs", a, i, self.rows[i], modes[part][i]) for i, a in enumerate(self.order)]
        middle = [] if last is None else [("ar", last, depth - 1, self.rows[-1], "direct")]
        gather = [("ag", a, i, rows, mode) for _, a, i, rows, mode in scatter[::-1]]
        self.stages = scatter + middle + gather
        self.final = len(scatter + middle) - 1
        self.first, self.slots, count = [], [], 0
        for kind, axis, pos, rows, mode in self.stages:
            n = AXES[axis][0]
            self.first.append(count)
            count += n - 1
            if kind != "ag":
                self.slots.append([held + s * rows for s in range(n - 1)])
                held += (n - 1) * rows
        self.count, self.held_end = count, held
        self.sums = [
            slots[-1 if self.stages[t][4] == "ring" else 0] for t, slots in enumerate(self.slots)
        ]
        self.events = []
        for g, (kind, axis, pos, rows, mode) in enumerate(self.stages):
            n = AXES[axis][0]
            after = self.initial(g + 1)
            if mode == "ring":
                for s in range(n - 1):
                    self.events.append(([(g, s)], (g, s), [(g, s + 1)] if s < n - 2 else after))
            else:
                self.events.append(([(g, s) for s in range(n - 1)], (g, None), after))

    def initial(self, g):
        if g >= len(self.stages):
            return []
        n = AXES[self.stages[g][1]][0]
        return [(g, 0)] if self.stages[g][4] == "ring" else [(g, s) for s in range(n - 1)]


class Plan:
    def __init__(self, rounds, latency=2.0, rate=47e3, extra=(), before=()):
        self.streams, held, base = [], 0, 0
        for number, (units, modes, delay) in enumerate(rounds):
            for part in range(3):
                for d in range(2):
                    length = units[part]
                    if not length:
                        continue
                    st = Stream(len(self.streams), part, (1, -1)[d], base, length, held, modes)
                    st.round, st.delay = number, delay
                    held = st.held_end
                    base += length
                    self.streams.append(st)
        self.held, self.rows = held, base
        self.copies = max(st.count for st in self.streams)
        self.simulate(latency, rate, extra, before)

    def simulate(self, latency, rate, extra=(), before=()):
        free, order, ready, core = {}, [], [], 0.0
        arrival = {}

        def send(st, copy, now):
            g, s = copy
            kind, axis, pos, rows, mode = st.stages[g]
            n = AXES[axis][0]
            hops, direction = 1, st.dir
            if mode == "direct":
                hops = min(s + 1, n - s - 1)
                direction = 1 if s + 1 <= n // 2 else -1
            link = (axis, direction)
            start = max(now, free.get(link, 0.0))
            free[link] = start + hops * rows * LANES * 4 / rate
            arrival[st.index, copy] = free[link] + latency + 0.8 * (hops - 1)

        nxt = {}
        for st in self.streams:
            nxt[st.index] = -1
        early = list(before)
        pieces, done0 = list(extra), len([s for s in self.streams if s.round == 0])
        self.round_end = {}
        while True:
            best = None
            for st in self.streams:
                e = nxt[st.index]
                if e >= len(st.events):
                    continue
                when = st.delay if e < 0 else max(arrival[st.index, c] for c in st.events[e][0])
                key = (max(when, core), st.round, when, st.index)
                if best is None or key < best[0]:
                    best = (key, st)
            if best is None:
                break
            if early and (best[0][0] > core + 0.3 or best[1].round > 0):
                core += early.pop(0)
                order.append(("early", None))
                continue
            if pieces and done0 == 0 and best[0][0] > core + 0.3:
                core += pieces.pop(0)
                order.append(("piece", None))
                continue
            when, st = best[0][0], best[1]
            e = nxt[st.index]
            core = when + 0.1
            order.append((st.index, e))
            for copy in (st.initial(0) if e < 0 else st.events[e][2]):
                send(st, copy, core)
            nxt[st.index] += 1
            if nxt[st.index] >= len(st.events):
                self.round_end[st.round] = core
                if st.round == 0:
                    done0 -= 1
                order.append(("end", st.index))
        for _ in pieces:
            order.append(("piece", None))
        self.order, self.time = order, core + sum(pieces)


def add_into(dst, dst_off, terms, rows):
    step = rows
    for cand in (192, 144, 128, 96, 72, 64):
        if rows > cand and rows % cand == 0:
            step = cand
            break

    def value(term, j):
        if isinstance(term[0], tuple):
            total = value(term[0], j)
            for other in term[1:]:
                total = total + value(other, j)
            return total
        ref, off = term
        return ref[pl.ds(aligned(off + j * step), step), :]

    def one(j, _):
        dst[pl.ds(aligned(dst_off + j * step), step), :] = value(terms, j)
        return 0

    if step == rows:
        one(0, 0)
    else:
        lax.fori_loop(0, rows // step, one, 0)


def aligned(v):
    return v if isinstance(v, int) else pl.multiple_of(v, 8)


class Ring:
    def __init__(self, plan, data_ref, out_ref, held, send_sem, recv_sem):
        self.plan, self.data, self.out, self.held = plan, data_ref, out_ref, held
        self.send_sem, self.recv_sem = send_sem, recv_sem
        self.r, self.here = coords()
        core = lax.axis_index("blk")
        self.chunks, self.ids, self.bases = {}, {}, {}
        for axis, (n, stride) in enumerate(AXES):
            for offset in range(n):
                k = lax.rem(self.here[axis] + offset, n) if offset else self.here[axis]
                self.chunks[axis, offset] = k
                self.ids[axis, offset] = 2 * (self.r + (k - self.here[axis]) * stride) + core

    def neighbour(self, axis, offset):
        return self.ids[axis, offset % AXES[axis][0]]

    def chunk(self, axis, offset):
        return self.chunks[axis, offset % AXES[axis][0]]

    def own(self, st, g, k):
        if g == 0:
            return self.data, aligned(st.base + k * st.rows[0])
        return self.held, aligned(st.sums[g - 1] + k * st.rows[g])

    def place(self, st, pos, k):
        if (st.index, pos) not in self.bases:
            off = st.base
            for i in range(pos):
                off = off + self.here[st.order[i]] * st.rows[i]
            self.bases[st.index, pos] = off
        return aligned(self.bases[st.index, pos] + k * st.rows[pos])

    def copy(self, st, copy, receive=False):
        g, s = copy
        kind, axis, pos, rows, mode = st.stages[g]
        ring = mode == "ring"
        target = st.dir if ring else s + 1
        if kind == "rs":
            if ring and s > 0:
                src = self.held, st.slots[g][s - 1]
            else:
                src = self.own(st, g, self.chunk(axis, -st.dir if ring else s + 1))
            dst = self.held, st.slots[g][s]
        elif kind == "ar":
            src = self.held, st.sums[g - 1]
            dst = self.held, st.slots[g][s]
        else:
            ahead = -st.dir * s if ring else 0
            back = -st.dir * (s + 1) if ring else -(s + 1)
            src = self.out, self.place(st, pos, self.chunk(axis, ahead))
            dst = self.out, self.place(st, pos, self.chunk(axis, back if receive else ahead))
        return pltpu.make_async_remote_copy(
            src_ref=src[0].at[pl.ds(src[1], rows), :],
            dst_ref=dst[0].at[pl.ds(dst[1], rows), :],
            send_sem=self.send_sem.at[st.index, st.first[g] + s],
            recv_sem=self.recv_sem.at[st.index, st.first[g] + s],
            device_id=self.neighbour(axis, target),
            device_id_type=LOGICAL,
        )

    def event(self, index, e):
        st = self.plan.streams[index]
        if e < 0:
            for c in st.initial(0):
                self.copy(st, c).start()
            return
        waits, (g, s), sends = st.events[e]
        for c in waits:
            self.copy(st, c, receive=True).wait_recv()
        kind, axis, pos, rows, mode = st.stages[g]
        if kind != "ag":
            final = g == st.final and s in (None, AXES[axis][0] - 2)
            if kind == "ar":
                a, b, c = [(self.held, slot) for slot in st.slots[g]]
                terms = (((self.held, st.sums[g - 1]), b), (a, c))
            elif s is None:
                own = self.own(st, g, self.chunk(axis, 0))
                terms = (own,) + tuple((self.held, slot) for slot in st.slots[g])
            else:
                own = self.own(st, g, self.chunk(axis, -st.dir * (s + 2)))
                terms = ((self.held, st.slots[g][s]), own)
            if final:
                dst = self.out, self.place(st, pos, self.chunk(axis if kind == "rs" else st.order[pos], 0))
            else:
                dst = self.held, st.slots[g][s or 0]
            add_into(*dst, terms, rows)
        for c in sends:
            self.copy(st, c).start()

    def finish(self):
        for st in self.plan.streams:
            for g in range(len(st.stages)):
                for s in range(AXES[st.stages[g][1]][0] - 1):
                    self.copy(st, (g, s)).wait_send()

    def devices(self):
        for axis, (n, _) in enumerate(AXES):
            for offset in range(1, n):
                yield self.neighbour(axis, offset)


LOW, HIGH_EIG = 0.05, 130.0
NEWTON = 8


def newton_scales():
    rho = (HIGH_EIG - LOW) / (HIGH_EIG + LOW)
    scales = []
    for _ in range(NEWTON + 1):
        scales.append(2.0 / (2.0 - rho * rho))
        rho = rho * rho / (2.0 - rho * rho)
    return scales


def mm(a, b):
    return jnp.dot(a, b, precision=HIGHEST, preferred_element_type=jnp.float32)


def split(value):
    high = value.astype(jnp.bfloat16)
    return high, (value - high.astype(jnp.float32)).astype(jnp.bfloat16)


class Inverses:
    def __init__(self, src, work, pivot):
        self.src, self.work, self.pivot = src, work, pivot
        self.scales = newton_scales()

    @staticmethod
    def durations():
        return [1.0] + SLABS * ([0.3] + (NEWTON // 2) * [1.4] + [0.8, 0.8])

    def pieces(self):
        yield self.load
        for k in range(SLABS):
            yield functools.partial(self.start, k)
            for i in range(NEWTON // 2):
                yield functools.partial(self.newton, k, i)
            for m in range(2):
                yield functools.partial(self.update, k, m)

    def eye(self):
        shape = (LANES, LANES)
        return lax.broadcasted_iota(jnp.int32, shape, 0) == lax.broadcasted_iota(jnp.int32, shape, 1)

    def load(self):
        eye = jnp.where(self.eye(), jnp.float32(ridge), jnp.float32(0.0))
        for m in range(2):
            for i in range(SLABS):
                for j in range(i + 1):
                    tile = self.src[pl.ds(tile_row(m, i, j), LANES), :]
                    a, b = slice(i * LANES, (i + 1) * LANES), slice(j * LANES, (j + 1) * LANES)
                    if i == j:
                        self.work[m, a, b] = tile + eye
                    else:
                        self.work[m, a, b] = tile
                        self.work[m, b, a] = tile.T

    def start(self, k):
        here = slice(k * LANES, (k + 1) * LANES)
        c, s = 2.0 / (LOW + HIGH_EIG), self.scales[0]
        for m in range(2):
            self.pivot[m] = jnp.where(self.eye(), jnp.float32(2.0 * c * s), jnp.float32(0.0)) - (c * c * s) * self.work[m, here, here]

    def newton(self, k, i):
        here = slice(k * LANES, (k + 1) * LANES)
        first, second = self.scales[1 + 2 * i], self.scales[2 + 2 * i]

        def step(t, _):
            s = jnp.where(t == 0, jnp.float32(first), jnp.float32(second))
            xs = [self.pivot[m] for m in range(2)]
            ax = [mm(self.work[m, here, here], xs[m]) for m in range(2)]
            xax = [mm(xs[m], ax[m]) for m in range(2)]
            for m in range(2):
                self.pivot[m] = s * (2.0 * xs[m] - xax[m])
            return 0

        lax.fori_loop(0, 2, step, 0)

    def update(self, k, m):
        here = slice(k * LANES, (k + 1) * LANES)
        work, inv = self.work, self.pivot[m]
        row = mm(inv, work[m, here, :])
        col = work[m, :, here]
        work[m, :, here] = jnp.zeros_like(col)
        work[m, here, :] = row
        work[m, here, here] = inv
        full = work[m, here, :]
        for i in range(SLABS):
            if i != k:
                rows = slice(i * LANES, (i + 1) * LANES)
                work[m, rows, :] = work[m, rows, :] - mm(col[rows], full)


def sum_kernel(plan, scale, xt_ref, proj_ref, phase_ref, y_ref, ft_hbm, sum_hbm, cross_hbm, high_hbm, low_hbm,
               ft_ref, out_ref, high_ref, low_ref, data_ref, held, work, pivot,
               send_sem, recv_sem, pair_send, pair_recv, feat_send, feat_recv, store_sem):
    ring = Ring(plan, data_ref, out_ref, held, send_sem, recv_sem)
    core = lax.axis_index("blk")
    other = 2 * ring.r + 1 - core
    barrier = pltpu.get_barrier_semaphore()
    met = 1
    pl.semaphore_signal(barrier, inc=1, device_id=other, device_id_type=LOGICAL)
    for device in ring.devices():
        pl.semaphore_signal(barrier, inc=1, device_id=device, device_id_type=LOGICAL)
        met += 1
    pl.semaphore_wait(barrier, met)

    def pair(slot, src, dst):
        return pltpu.make_async_remote_copy(
            src_ref=src, dst_ref=dst, send_sem=pair_send.at[slot], recv_sem=pair_recv.at[slot],
            device_id=other, device_id_type=LOGICAL,
        )

    crossing = [st for st in plan.streams if CROSS <= st.base and st.base + st.length <= MOMENT]
    assert sum(st.length for st in crossing) == MOMENT - CROSS and len(crossing) == 4

    def cross(slot):
        st = crossing[slot]
        rows = st.length
        return pair(2 + slot, out_ref.at[pl.ds(st.base, rows), :], cross_hbm.at[pl.ds(st.base - CROSS, rows), :])

    stores = []

    def store(src, dst):
        stores.append(pltpu.make_async_copy(src, dst, store_sem.at[len(stores)]))
        stores[-1].start()

    parts = Parts(scale, xt_ref, proj_ref, phase_ref, y_ref, ft_ref, data_ref, feat_send, feat_recv)
    parts.first()
    for i in range(2):
        store(ft_ref.at[parts.own[i]], ft_hbm.at[parts.own[i]])
    early = parts.rest()
    inverses = Inverses(out_ref, work, pivot)
    pieces = inverses.pieces()
    for what, arg in plan.order:
        if what == "piece":
            next(pieces)()
        elif what == "early":
            next(early)()
        elif what == "end":
            st = plan.streams[arg]
            rows = pl.ds(st.base, st.length)
            store(out_ref.at[rows, :], sum_hbm.at[rows, :])
            if st in crossing:
                cross(crossing.index(st)).start()
        else:
            ring.event(what, arg)
    for i in range(2):
        store(ft_ref.at[parts.other[i]], ft_hbm.at[parts.other[i]])
    mine, theirs = pl.ds(2 * core, 2), pl.ds(2 * (1 - core), 2)
    for m in range(2):
        high_ref[m], low_ref[m] = split(work[m])
    for k, (ref, dst) in enumerate(((high_ref, high_hbm), (low_ref, low_hbm))):
        pair(k, ref, dst.at[mine]).start()
        store(ref, dst.at[mine])
    ring.finish()
    parts.finish()
    for slot in range(len(crossing)):
        cross(slot).wait()
    for k, (ref, dst) in enumerate(((high_ref, high_hbm), (low_ref, low_hbm))):
        pair(k, ref, dst.at[theirs]).wait()
    for copy in stores:
        copy.wait()


def mode(first, second, middle):
    return ((first, second, "direct"), (middle, "direct"), (first, second, "direct"))


ROUNDS = (
    ((1024, 256, 1024), mode("ring", "direct", "ring"), 0.0),
    ((2048, 2048, 2048), mode("ring", "ring", "ring"), 7.0),
)


def sum_and_invert(xt, proj, phase, y):
    rows = xt.shape[1]
    scale = 1.0 / math.sqrt(rows * 128)
    plan = Plan(ROUNDS, extra=Inverses.durations(), before=Parts.durations())
    assert plan.rows == DATA_ROWS
    vmem = pl.BlockSpec(memory_space=pltpu.VMEM)
    sems = pltpu.SemaphoreType.DMA((len(plan.streams), plan.copies))
    return pl.pallas_call(
        functools.partial(sum_kernel, plan, scale),
        out_shape=(
            jax.ShapeDtypeStruct((4, F, rows), jnp.bfloat16),
            jax.ShapeDtypeStruct((DATA_ROWS, LANES), jnp.float32),
            jax.ShapeDtypeStruct((3 * SLABS * F, LANES), jnp.float32),
            jax.ShapeDtypeStruct((4, F, F), jnp.bfloat16),
            jax.ShapeDtypeStruct((4, F, F), jnp.bfloat16),
        ),
        in_specs=[vmem] * 4,
        out_specs=(pl.BlockSpec(memory_space=pl.ANY),) * 5,
        scratch_shapes=[
            pltpu.VMEM((4, F, rows), jnp.bfloat16),
            pltpu.VMEM((DATA_ROWS, LANES), jnp.float32),
            pltpu.VMEM((2, F, F), jnp.bfloat16),
            pltpu.VMEM((2, F, F), jnp.bfloat16),
            pltpu.VMEM((DATA_ROWS, LANES), jnp.float32),
            pltpu.VMEM((plan.held, LANES), jnp.float32),
            pltpu.VMEM((2, F, F), jnp.float32),
            pltpu.VMEM((2, LANES, LANES), jnp.float32),
            sems,
            sems,
            pltpu.SemaphoreType.DMA((6,)),
            pltpu.SemaphoreType.DMA((6,)),
            pltpu.SemaphoreType.DMA((2,)),
            pltpu.SemaphoreType.DMA((2,)),
            pltpu.SemaphoreType.DMA((len(plan.streams) + 6,)),
        ],
        compiler_params=pltpu.CompilerParams(
            collective_id=1, has_side_effects=True, vmem_limit_bytes=60 * 2**20
        ),
        name="sum_and_invert",
    )(xt, proj, phase, y)


def dot(a, b):
    return jnp.dot(a, b, preferred_element_type=jnp.float32)


def sweep_kernel(sum_ref, cross_ref, ih, il, ft_ref, y_ref, coef_ref, res_ref, gh, gl):
    core = lax.axis_index("blk")
    for own, (gref, base) in enumerate(((sum_ref, CROSS), (cross_ref, 0))):
        owner = core if own == 0 else 1 - core
        for k in range(3):
            for j in range(SLABS):
                high, low = split(gref[pl.ds(base + (k * SLABS + j) * F, F), :])
                cols = slice(j * LANES, (j + 1) * LANES)
                gh[3 * owner + k, :, cols] = high
                gl[3 * owner + k, :, cols] = low
    where = {(1, 0): 0, (2, 0): 1, (3, 1): 2, (3, 2): 3, (2, 1): 4, (3, 0): 5}

    def one(half, _):
        cols = pl.ds(pl.multiple_of(half * 256, 256), 256)
        rounded = []
        for b in range(4):
            corr = jnp.concatenate(
                [
                    sum_ref[pl.ds(pl.multiple_of(MOMENT + (b * SLABS + 2 * half + k) * F, F), F), :]
                    for k in range(2)
                ],
                axis=1,
            )
            for j in range(b):
                corr = corr - (dot(gh[where[b, j]], rounded[j]) + dot(gl[where[b, j]], rounded[j]))
            ch, cl = split(corr)
            delta = dot(ih[b], ch) + (dot(ih[b], cl) + dot(il[b], ch))
            coef_ref[b, :, cols] = delta
            rounded.append(delta.astype(jnp.bfloat16))
        fit = lax.dot_general(
            ft_ref[0], rounded[0], (((0,), (0,)), ((), ())), preferred_element_type=jnp.float32
        )
        for b in range(1, 4):
            fit = fit + lax.dot_general(
                ft_ref[b], rounded[b], (((0,), (0,)), ((), ())), preferred_element_type=jnp.float32
            )
        res_ref[:, cols] = y_ref[:, cols].astype(jnp.float32) - fit
        return 0

    lax.fori_loop(0, 2, one, 0)


def sweep(summed, cross, high, low, ft, y):
    vmem = pl.BlockSpec(memory_space=pltpu.VMEM)
    return pl.pallas_call(
        sweep_kernel,
        out_shape=(
            jax.ShapeDtypeStruct((4, F, y.shape[1]), jnp.float32),
            jax.ShapeDtypeStruct(y.shape, jnp.float32),
        ),
        in_specs=[vmem] * 6,
        out_specs=(vmem, vmem),
        scratch_shapes=[pltpu.VMEM((6, F, F), jnp.bfloat16), pltpu.VMEM((6, F, F), jnp.bfloat16)],
        compiler_params=pltpu.CompilerParams(vmem_limit_bytes=60 * 2**20),
        name="sweep",
    )(summed, cross, high, low, ft, y)


def body(inputs, proj, phase, targets):
    ft, summed, cross, high, low = sum_and_invert(jnp.swapaxes(inputs, 0, 1), proj, phase, targets)
    return sweep(summed, cross, high, low, ft, targets)


def solution(mesh):
    return jax.shard_map(
        body,
        mesh=mesh,
        in_specs=(P("rows", None), P("blk", None, None), P("blk", None), P("rows", "blk")),
        out_specs=(P(None, None, "blk"), P("rows", "blk")),
        check_vma=False,
    )
```

```python
import functools
import math

import jax
import jax.numpy as jnp
from jax import lax
from jax.experimental import pallas as pl
from jax.experimental.pallas import tpu as pltpu
from jax.sharding import PartitionSpec as P

MESH = pl.DeviceIdType.MESH
LOGICAL = pl.DeviceIdType.LOGICAL
HIGHEST = lax.Precision.HIGHEST
ridge = 0.05

F = 512
LANES = 128
SLABS = F // LANES
TILES = SLABS * (SLABS + 1) // 2
CROSS = 2 * TILES * LANES
MOMENT = CROSS + 3 * SLABS * F
DATA_ROWS = MOMENT + 4 * SLABS * F


def tile_row(m, i, j):
    return (m * TILES + i * (i + 1) // 2 + j) * LANES


def sibling():
    return {"blk": 1 - lax.axis_index("blk")}


def cos_turns(t):
    u = jnp.abs(t) - 0.25
    w = u * u
    acc = jnp.full_like(w, SIN_POLY[-1])
    for coef in SIN_POLY[-2::-1]:
        acc = acc * w + coef
    return acc * u


def fit_sin_poly():
    import numpy as np

    degree = 5
    nodes = (np.cos((np.arange(degree + 1) + 0.5) * np.pi / (degree + 1)) + 1.0) / 32.0
    root = np.sqrt(nodes)
    values = -np.sin(2 * np.pi * root) / root
    vander = np.vander(nodes, degree + 1, increasing=True)
    return [float(v) for v in np.linalg.solve(vander, values)]


SIN_POLY = fit_sin_poly()


class Parts:
    def __init__(self, scale, xt_ref, proj_ref, phase_ref, y_ref, ft_ref, part_ref, send_sem, recv_sem):
        self.scale, self.xt, self.proj, self.phase, self.y = scale, xt_ref, proj_ref, phase_ref, y_ref
        self.ft, self.part, self.send_sem, self.recv_sem = ft_ref, part_ref, send_sem, recv_sem
        self.core = lax.axis_index("blk")
        self.own = [2 * self.core, 2 * self.core + 1]
        self.other = [2 * (1 - self.core), 2 * (1 - self.core) + 1]

    def exchange(self, i, receive=False):
        return pltpu.make_async_remote_copy(
            src_ref=self.ft.at[self.own[i]],
            dst_ref=self.ft.at[(self.other if receive else self.own)[i]],
            send_sem=self.send_sem.at[i],
            recv_sem=self.recv_sem.at[i],
            device_id=sibling(),
            device_id_type=MESH,
        )

    def features(self, i):
        chunk = 256
        shift = jnp.broadcast_to(self.phase[i:i + 1, :].astype(jnp.float32), (8, F)).T[:, :1]

        def piece(j, _):
            cols = pl.ds(pl.multiple_of(j * chunk, chunk), chunk)
            pre = lax.dot_general(
                self.proj[i], self.xt[:, cols], (((0,), (0,)), ((), ())), preferred_element_type=jnp.float32
            )
            turns = (pre + shift) * (0.5 / math.pi)
            turns = turns - jnp.round(turns)
            self.ft[self.own[i], :, cols] = (cos_turns(turns) * self.scale).astype(jnp.bfloat16)
            return 0

        lax.fori_loop(0, self.xt.shape[1] // chunk, piece, 0)
        self.exchange(i).start()

    def put(self, base, half, value):
        for k in range(2):
            row = pl.multiple_of(base + (2 * half + k) * F, LANES)
            self.part[pl.ds(row, F), :] = value[:, k * LANES:(k + 1) * LANES]

    def diagonal(self, m):
        a = self.own[m]
        for half in range(2):
            top = 256 * half
            value = lax.dot_general(
                self.ft[a, top:, :], self.ft[a, top:top + 256, :], (((1,), (1,)), ((), ())),
                preferred_element_type=jnp.float32,
            )
            for k in range(2):
                j = 2 * half + k
                for i in range(j, SLABS):
                    rows = slice(i * LANES - top, (i + 1) * LANES - top)
                    self.part[pl.ds(tile_row(m, i, j), LANES), :] = value[rows, k * LANES:(k + 1) * LANES]

    def gram(self, q, a, b):
        def one(half, _):
            cols = pl.ds(pl.multiple_of(half * 256, 256), 256)
            self.put(CROSS + q * SLABS * F, half, lax.dot_general(
                self.ft[a], self.ft[b, cols, :], (((1,), (1,)), ((), ())), preferred_element_type=jnp.float32
            ))
            return 0

        lax.fori_loop(0, 2, one, 0)

    def moment(self, b):
        def one(half, _):
            cols = pl.ds(pl.multiple_of(half * 256, 256), 256)
            self.put(MOMENT + b * SLABS * F, half, jnp.dot(
                self.ft[b], self.y[:, cols], preferred_element_type=jnp.float32
            ))
            return 0

        lax.fori_loop(0, 2, one, 0)

    def first(self):
        for i in range(2):
            self.features(i)
        for i in range(2):
            self.diagonal(i)
        self.gram(0, self.own[1], self.own[0])

    @staticmethod
    def durations():
        return [1.0] * 6

    def rest(self):
        yield functools.partial(self.moment, self.own[0])
        yield functools.partial(self.moment, self.own[1])

        def crossed():
            for i in range(2):
                self.exchange(i, receive=True).wait_recv()
            self.gram(1, 2, self.core)

        yield crossed
        yield functools.partial(self.gram, 2, 3, 1 - self.core)
        yield functools.partial(self.moment, self.other[0])
        yield functools.partial(self.moment, self.other[1])

    def finish(self):
        for i in range(2):
            self.exchange(i).wait_send()


AXES = ((4, 32), (8, 4), (4, 1))
Y, Z, X = 0, 1, 2
PARTS = (((Y, X, Z), None), ((Z, X), Y), ((X, Y, Z), None))


def coords():
    r = lax.axis_index("rows")
    return r, [lax.rem(r // stride, n) for n, stride in AXES]


class Stream:
    def __init__(self, index, part, direction, base, length, held, modes):
        self.index, self.dir, self.base, self.length = index, direction, base, length
        self.order, last = PARTS[part]
        depth = len(self.order)
        self.rows = []
        for a in self.order:
            length //= AXES[a][0]
            self.rows.append(length)
        assert length % 8 == 0
        scatter = [("rs", a, i, self.rows[i], modes[part][i]) for i, a in enumerate(self.order)]
        middle = [] if last is None else [("ar", last, depth - 1, self.rows[-1], "direct")]
        gather = [("ag", a, i, rows, mode) for _, a, i, rows, mode in scatter[::-1]]
        self.stages = scatter + middle + gather
        self.final = len(scatter + middle) - 1
        self.first, self.slots, count = [], [], 0
        for kind, axis, pos, rows, mode in self.stages:
            n = AXES[axis][0]
            self.first.append(count)
            count += n - 1
            if kind != "ag":
                self.slots.append([held + s * rows for s in range(n - 1)])
                held += (n - 1) * rows
        self.count, self.held_end = count, held
        self.sums = [
            slots[-1 if self.stages[t][4] == "ring" else 0] for t, slots in enumerate(self.slots)
        ]
        self.events = []
        for g, (kind, axis, pos, rows, mode) in enumerate(self.stages):
            n = AXES[axis][0]
            after = self.initial(g + 1)
            if mode == "ring":
                for s in range(n - 1):
                    self.events.append(([(g, s)], (g, s), [(g, s + 1)] if s < n - 2 else after))
            else:
                self.events.append(([(g, s) for s in range(n - 1)], (g, None), after))

    def initial(self, g):
        if g >= len(self.stages):
            return []
        n = AXES[self.stages[g][1]][0]
        return [(g, 0)] if self.stages[g][4] == "ring" else [(g, s) for s in range(n - 1)]


class Plan:
    def __init__(self, rounds, latency=2.4, rate=47e3, extra=(), before=()):
        self.streams, held, base = [], 0, 0
        for number, (units, modes, delay) in enumerate(rounds):
            for part in range(3):
                for d in range(2):
                    length = units[part]
                    if not length:
                        continue
                    st = Stream(len(self.streams), part, (1, -1)[d], base, length, held, modes)
                    st.round, st.delay = number, delay
                    held = st.held_end
                    base += length
                    self.streams.append(st)
        self.held, self.rows = held, base
        self.copies = max(st.count for st in self.streams)
        self.simulate(latency, rate, extra, before)

    def simulate(self, latency, rate, extra=(), before=()):
        free, order, ready, core = {}, [], [], 0.0
        arrival = {}

        def send(st, copy, now):
            g, s = copy
            kind, axis, pos, rows, mode = st.stages[g]
            n = AXES[axis][0]
            hops, direction = 1, st.dir
            if mode == "direct":
                hops = min(s + 1, n - s - 1)
                direction = 1 if s + 1 <= n // 2 else -1
            link = (axis, direction)
            start = max(now, free.get(link, 0.0))
            free[link] = start + hops * rows * LANES * 4 / rate
            arrival[st.index, copy] = free[link] + latency + 0.8 * (hops - 1)

        nxt = {}
        for st in self.streams:
            nxt[st.index] = -1
        early = list(before)
        pieces, done0 = list(extra), len([s for s in self.streams if s.round == 0])
        self.round_end = {}
        while True:
            best = None
            for st in self.streams:
                e = nxt[st.index]
                if e >= len(st.events):
                    continue
                when = st.delay if e < 0 else max(arrival[st.index, c] for c in st.events[e][0])
                key = (max(when, core), st.round, when, st.index)
                if best is None or key < best[0]:
                    best = (key, st)
            if best is None:
                break
            if early and (best[0][0] > core + 0.3 or best[1].round > 0):
                core += early.pop(0)
                order.append(("early", None))
                continue
            if pieces and done0 == 0 and best[0][0] > core + 0.3:
                core += pieces.pop(0)
                order.append(("piece", None))
                continue
            when, st = best[0][0], best[1]
            e = nxt[st.index]
            core = when + 0.1
            order.append((st.index, e))
            for copy in (st.initial(0) if e < 0 else st.events[e][2]):
                send(st, copy, core)
            nxt[st.index] += 1
            if nxt[st.index] >= len(st.events):
                self.round_end[st.round] = core
                if st.round == 0:
                    done0 -= 1
                order.append(("end", st.index))
        for _ in pieces:
            order.append(("piece", None))
        self.order, self.time = order, core + sum(pieces)


def add_into(dst, dst_off, terms, rows):
    step = rows
    for cand in (192, 144, 128, 96, 72, 64):
        if rows > cand and rows % cand == 0:
            step = cand
            break

    def value(term, j):
        if isinstance(term[0], tuple):
            total = value(term[0], j)
            for other in term[1:]:
                total = total + value(other, j)
            return total
        ref, off = term
        return ref[pl.ds(aligned(off + j * step), step), :]

    def one(j, _):
        dst[pl.ds(aligned(dst_off + j * step), step), :] = value(terms, j)
        return 0

    if step == rows:
        one(0, 0)
    else:
        lax.fori_loop(0, rows // step, one, 0)


def aligned(v):
    return v if isinstance(v, int) else pl.multiple_of(v, 8)


class Ring:
    def __init__(self, plan, data_ref, out_ref, held, send_sem, recv_sem):
        self.plan, self.data, self.out, self.held = plan, data_ref, out_ref, held
        self.send_sem, self.recv_sem = send_sem, recv_sem
        self.r, self.here = coords()
        core = lax.axis_index("blk")
        self.chunks, self.ids, self.bases = {}, {}, {}
        for axis, (n, stride) in enumerate(AXES):
            for offset in range(n):
                k = lax.rem(self.here[axis] + offset, n) if offset else self.here[axis]
                self.chunks[axis, offset] = k
                self.ids[axis, offset] = 2 * (self.r + (k - self.here[axis]) * stride) + core

    def neighbour(self, axis, offset):
        return self.ids[axis, offset % AXES[axis][0]]

    def chunk(self, axis, offset):
        return self.chunks[axis, offset % AXES[axis][0]]

    def own(self, st, g, k):
        if g == 0:
            return self.data, aligned(st.base + k * st.rows[0])
        return self.held, aligned(st.sums[g - 1] + k * st.rows[g])

    def place(self, st, pos, k):
        if (st.index, pos) not in self.bases:
            off = st.base
            for i in range(pos):
                off = off + self.here[st.order[i]] * st.rows[i]
            self.bases[st.index, pos] = off
        return aligned(self.bases[st.index, pos] + k * st.rows[pos])

    def copy(self, st, copy, receive=False):
        g, s = copy
        kind, axis, pos, rows, mode = st.stages[g]
        ring = mode == "ring"
        target = st.dir if ring else s + 1
        if kind == "rs":
            if ring and s > 0:
                src = self.held, st.slots[g][s - 1]
            else:
                src = self.own(st, g, self.chunk(axis, -st.dir if ring else s + 1))
            dst = self.held, st.slots[g][s]
        elif kind == "ar":
            src = self.held, st.sums[g - 1]
            dst = self.held, st.slots[g][s]
        else:
            ahead = -st.dir * s if ring else 0
            back = -st.dir * (s + 1) if ring else -(s + 1)
            src = self.out, self.place(st, pos, self.chunk(axis, ahead))
            dst = self.out, self.place(st, pos, self.chunk(axis, back if receive else ahead))
        return pltpu.make_async_remote_copy(
            src_ref=src[0].at[pl.ds(src[1], rows), :],
            dst_ref=dst[0].at[pl.ds(dst[1], rows), :],
            send_sem=self.send_sem.at[st.index, st.first[g] + s],
            recv_sem=self.recv_sem.at[st.index, st.first[g] + s],
            device_id=self.neighbour(axis, target),
            device_id_type=LOGICAL,
        )

    def event(self, index, e):
        st = self.plan.streams[index]
        if e < 0:
            for c in st.initial(0):
                self.copy(st, c).start()
            return
        waits, (g, s), sends = st.events[e]
        for c in waits:
            self.copy(st, c, receive=True).wait_recv()
        kind, axis, pos, rows, mode = st.stages[g]
        if kind != "ag":
            final = g == st.final and s in (None, AXES[axis][0] - 2)
            if kind == "ar":
                a, b, c = [(self.held, slot) for slot in st.slots[g]]
                terms = (((self.held, st.sums[g - 1]), b), (a, c))
            elif s is None:
                own = self.own(st, g, self.chunk(axis, 0))
                terms = (own,) + tuple((self.held, slot) for slot in st.slots[g])
            else:
                own = self.own(st, g, self.chunk(axis, -st.dir * (s + 2)))
                terms = ((self.held, st.slots[g][s]), own)
            if final:
                dst = self.out, self.place(st, pos, self.chunk(axis if kind == "rs" else st.order[pos], 0))
            else:
                dst = self.held, st.slots[g][s or 0]
            add_into(*dst, terms, rows)
        for c in sends:
            self.copy(st, c).start()

    def finish(self):
        for st in self.plan.streams:
            for g in range(len(st.stages)):
                for s in range(AXES[st.stages[g][1]][0] - 1):
                    self.copy(st, (g, s)).wait_send()

    def devices(self):
        for axis, (n, _) in enumerate(AXES):
            for offset in range(1, n):
                yield self.neighbour(axis, offset)


LOW, HIGH_EIG = 0.05, 130.0
NEWTON = 8


def newton_scales():
    rho = (HIGH_EIG - LOW) / (HIGH_EIG + LOW)
    scales = []
    for _ in range(NEWTON + 1):
        scales.append(2.0 / (2.0 - rho * rho))
        rho = rho * rho / (2.0 - rho * rho)
    return scales


def mm(a, b):
    return jnp.dot(a, b, precision=HIGHEST, preferred_element_type=jnp.float32)


def split(value):
    high = value.astype(jnp.bfloat16)
    return high, (value - high.astype(jnp.float32)).astype(jnp.bfloat16)


class Inverses:
    def __init__(self, src, work, pivot):
        self.src, self.work, self.pivot = src, work, pivot
        self.scales = newton_scales()

    @staticmethod
    def durations():
        return [1.0] + SLABS * ([0.3] + (NEWTON // 2) * [1.4] + [0.8, 0.8])

    def pieces(self):
        yield self.load
        for k in range(SLABS):
            yield functools.partial(self.start, k)
            for i in range(NEWTON // 2):
                yield functools.partial(self.newton, k, i)
            for m in range(2):
                yield functools.partial(self.update, k, m)

    def eye(self):
        shape = (LANES, LANES)
        return lax.broadcasted_iota(jnp.int32, shape, 0) == lax.broadcasted_iota(jnp.int32, shape, 1)

    def load(self):
        eye = jnp.where(self.eye(), jnp.float32(ridge), jnp.float32(0.0))
        for m in range(2):
            for i in range(SLABS):
                for j in range(i + 1):
                    tile = self.src[pl.ds(tile_row(m, i, j), LANES), :]
                    a, b = slice(i * LANES, (i + 1) * LANES), slice(j * LANES, (j + 1) * LANES)
                    if i == j:
                        self.work[m, a, b] = tile + eye
                    else:
                        self.work[m, a, b] = tile
                        self.work[m, b, a] = tile.T

    def start(self, k):
        here = slice(k * LANES, (k + 1) * LANES)
        c, s = 2.0 / (LOW + HIGH_EIG), self.scales[0]
        for m in range(2):
            self.pivot[m] = jnp.where(self.eye(), jnp.float32(2.0 * c * s), jnp.float32(0.0)) - (c * c * s) * self.work[m, here, here]

    def newton(self, k, i):
        here = slice(k * LANES, (k + 1) * LANES)
        first, second = self.scales[1 + 2 * i], self.scales[2 + 2 * i]

        def step(t, _):
            s = jnp.where(t == 0, jnp.float32(first), jnp.float32(second))
            xs = [self.pivot[m] for m in range(2)]
            ax = [mm(self.work[m, here, here], xs[m]) for m in range(2)]
            xax = [mm(xs[m], ax[m]) for m in range(2)]
            for m in range(2):
                self.pivot[m] = s * (2.0 * xs[m] - xax[m])
            return 0

        lax.fori_loop(0, 2, step, 0)

    def update(self, k, m):
        here = slice(k * LANES, (k + 1) * LANES)
        work, inv = self.work, self.pivot[m]
        row = mm(inv, work[m, here, :])
        col = work[m, :, here]
        work[m, :, here] = jnp.zeros_like(col)
        work[m, here, :] = row
        work[m, here, here] = inv
        full = work[m, here, :]
        for i in range(SLABS):
            if i != k:
                rows = slice(i * LANES, (i + 1) * LANES)
                work[m, rows, :] = work[m, rows, :] - mm(col[rows], full)


def sum_kernel(plan, scale, xt_ref, proj_ref, phase_ref, y_ref, ft_hbm, sum_hbm, cross_hbm, high_hbm, low_hbm,
               ft_ref, out_ref, high_ref, low_ref, data_ref, held, work, pivot,
               send_sem, recv_sem, pair_send, pair_recv, feat_send, feat_recv, store_sem):
    ring = Ring(plan, data_ref, out_ref, held, send_sem, recv_sem)
    core = lax.axis_index("blk")
    other = 2 * ring.r + 1 - core
    barrier = pltpu.get_barrier_semaphore()
    met = 1
    pl.semaphore_signal(barrier, inc=1, device_id=other, device_id_type=LOGICAL)
    for device in ring.devices():
        pl.semaphore_signal(barrier, inc=1, device_id=device, device_id_type=LOGICAL)
        met += 1
    pl.semaphore_wait(barrier, met)

    def pair(slot, src, dst):
        return pltpu.make_async_remote_copy(
            src_ref=src, dst_ref=dst, send_sem=pair_send.at[slot], recv_sem=pair_recv.at[slot],
            device_id=other, device_id_type=LOGICAL,
        )

    crossing = [st for st in plan.streams if CROSS <= st.base and st.base + st.length <= MOMENT]
    assert sum(st.length for st in crossing) == MOMENT - CROSS and len(crossing) == 4

    def cross(slot):
        st = crossing[slot]
        rows = st.length
        return pair(2 + slot, out_ref.at[pl.ds(st.base, rows), :], cross_hbm.at[pl.ds(st.base - CROSS, rows), :])

    stores = []

    def store(src, dst):
        stores.append(pltpu.make_async_copy(src, dst, store_sem.at[len(stores)]))
        stores[-1].start()

    parts = Parts(scale, xt_ref, proj_ref, phase_ref, y_ref, ft_ref, data_ref, feat_send, feat_recv)
    parts.first()
    for i in range(2):
        store(ft_ref.at[parts.own[i]], ft_hbm.at[parts.own[i]])
    early = parts.rest()
    inverses = Inverses(out_ref, work, pivot)
    pieces = inverses.pieces()
    for what, arg in plan.order:
        if what == "piece":
            next(pieces)()
        elif what == "early":
            next(early)()
        elif what == "end":
            st = plan.streams[arg]
            rows = pl.ds(st.base, st.length)
            store(out_ref.at[rows, :], sum_hbm.at[rows, :])
            if st in crossing:
                cross(crossing.index(st)).start()
        else:
            ring.event(what, arg)
    for i in range(2):
        store(ft_ref.at[parts.other[i]], ft_hbm.at[parts.other[i]])
    mine, theirs = pl.ds(2 * core, 2), pl.ds(2 * (1 - core), 2)
    for m in range(2):
        high_ref[m], low_ref[m] = split(work[m])
    for k, (ref, dst) in enumerate(((high_ref, high_hbm), (low_ref, low_hbm))):
        pair(k, ref, dst.at[mine]).start()
        store(ref, dst.at[mine])
    ring.finish()
    parts.finish()
    for slot in range(len(crossing)):
        cross(slot).wait()
    for k, (ref, dst) in enumerate(((high_ref, high_hbm), (low_ref, low_hbm))):
        pair(k, ref, dst.at[theirs]).wait()
    for copy in stores:
        copy.wait()


def mode(first, second, middle):
    return ((first, second, "direct"), (middle, "direct"), (first, second, "direct"))


ROUNDS = (
    ((1024, 256, 1024), mode("ring", "direct", "ring"), 0.0),
    ((2048, 2048, 2048), mode("ring", "ring", "ring"), 7.0),
)


def sum_and_invert(xt, proj, phase, y):
    rows = xt.shape[1]
    scale = 1.0 / math.sqrt(rows * 128)
    plan = Plan(ROUNDS, extra=Inverses.durations(), before=Parts.durations())
    assert plan.rows == DATA_ROWS
    vmem = pl.BlockSpec(memory_space=pltpu.VMEM)
    sems = pltpu.SemaphoreType.DMA((len(plan.streams), plan.copies))
    return pl.pallas_call(
        functools.partial(sum_kernel, plan, scale),
        out_shape=(
            jax.ShapeDtypeStruct((4, F, rows), jnp.bfloat16),
            jax.ShapeDtypeStruct((DATA_ROWS, LANES), jnp.float32),
            jax.ShapeDtypeStruct((3 * SLABS * F, LANES), jnp.float32),
            jax.ShapeDtypeStruct((4, F, F), jnp.bfloat16),
            jax.ShapeDtypeStruct((4, F, F), jnp.bfloat16),
        ),
        in_specs=[vmem] * 4,
        out_specs=(pl.BlockSpec(memory_space=pl.ANY),) * 5,
        scratch_shapes=[
            pltpu.VMEM((4, F, rows), jnp.bfloat16),
            pltpu.VMEM((DATA_ROWS, LANES), jnp.float32),
            pltpu.VMEM((2, F, F), jnp.bfloat16),
            pltpu.VMEM((2, F, F), jnp.bfloat16),
            pltpu.VMEM((DATA_ROWS, LANES), jnp.float32),
            pltpu.VMEM((plan.held, LANES), jnp.float32),
            pltpu.VMEM((2, F, F), jnp.float32),
            pltpu.VMEM((2, LANES, LANES), jnp.float32),
            sems,
            sems,
            pltpu.SemaphoreType.DMA((6,)),
            pltpu.SemaphoreType.DMA((6,)),
            pltpu.SemaphoreType.DMA((2,)),
            pltpu.SemaphoreType.DMA((2,)),
            pltpu.SemaphoreType.DMA((len(plan.streams) + 6,)),
        ],
        compiler_params=pltpu.CompilerParams(
            collective_id=1, has_side_effects=True, vmem_limit_bytes=60 * 2**20
        ),
        name="sum_and_invert",
    )(xt, proj, phase, y)


def dot(a, b):
    return jnp.dot(a, b, preferred_element_type=jnp.float32)


def sweep_kernel(sum_ref, cross_ref, ih, il, ft_ref, y_ref, coef_ref, res_ref, gh, gl):
    core = lax.axis_index("blk")
    half = pl.program_id(0)

    @pl.when(half == 0)
    def _():
        for own, (gref, base) in enumerate(((sum_ref, CROSS), (cross_ref, 0))):
            owner = core if own == 0 else 1 - core
            for k in range(3):
                for j in range(SLABS):
                    high, low = split(gref[pl.ds(base + (k * SLABS + j) * F, F), :])
                    cols = slice(j * LANES, (j + 1) * LANES)
                    gh[3 * owner + k, :, cols] = high
                    gl[3 * owner + k, :, cols] = low

    where = {(1, 0): 0, (2, 0): 1, (3, 1): 2, (3, 2): 3, (2, 1): 4, (3, 0): 5}
    rounded = []
    for b in range(4):
        corr = jnp.concatenate(
            [
                sum_ref[pl.ds(pl.multiple_of(MOMENT + (b * SLABS + 2 * half + k) * F, F), F), :]
                for k in range(2)
            ],
            axis=1,
        )
        for j in range(b):
            corr = corr - (dot(gh[where[b, j]], rounded[j]) + dot(gl[where[b, j]], rounded[j]))
        ch, cl = split(corr)
        delta = dot(ih[b], ch) + (dot(ih[b], cl) + dot(il[b], ch))
        coef_ref[b] = delta
        rounded.append(delta.astype(jnp.bfloat16))
    fit = lax.dot_general(
        ft_ref[0], rounded[0], (((0,), (0,)), ((), ())), preferred_element_type=jnp.float32
    )
    for b in range(1, 4):
        fit = fit + lax.dot_general(
            ft_ref[b], rounded[b], (((0,), (0,)), ((), ())), preferred_element_type=jnp.float32
        )
    res_ref[...] = y_ref[...].astype(jnp.float32) - fit


def sweep(summed, cross, high, low, ft, y):
    rows, cols = y.shape

    def whole(array):
        return pl.BlockSpec(array.shape, lambda i: (0,) * array.ndim, pipeline_mode=pl.Buffered(1))

    return pl.pallas_call(
        sweep_kernel,
        grid=(2,),
        out_shape=(
            jax.ShapeDtypeStruct((4, F, cols), jnp.float32),
            jax.ShapeDtypeStruct(y.shape, jnp.float32),
        ),
        in_specs=[whole(v) for v in (summed, cross, high, low, ft)]
        + [pl.BlockSpec((rows, cols // 2), lambda i: (0, i))],
        out_specs=(
            pl.BlockSpec((4, F, cols // 2), lambda i: (0, 0, i)),
            pl.BlockSpec((rows, cols // 2), lambda i: (0, i)),
        ),
        scratch_shapes=[pltpu.VMEM((6, F, F), jnp.bfloat16), pltpu.VMEM((6, F, F), jnp.bfloat16)],
        compiler_params=pltpu.CompilerParams(vmem_limit_bytes=60 * 2**20),
        name="sweep",
    )(summed, cross, high, low, ft, y)


def body(inputs, proj, phase, targets):
    ft, summed, cross, high, low = sum_and_invert(jnp.swapaxes(inputs, 0, 1), proj, phase, targets)
    return sweep(summed, cross, high, low, ft, targets)


def solution(mesh):
    return jax.shard_map(
        body,
        mesh=mesh,
        in_specs=(P("rows", None), P("blk", None, None), P("blk", None), P("rows", "blk")),
        out_specs=(P(None, None, "blk"), P("rows", "blk")),
        check_vma=False,
    )
```
